128 devices in a mesh: dp: 16 (over z, x_lo, core), ctx: 8 (over x_hi, y).
Axes of the slice: x: 4 (x_hi: 2, x_lo: 2; x = x_hi * 2 + x_lo), y: 4, z: 4, core: 2. Of those that a mesh axis runs over, the one named last changes fastest.
Arguments:
- hidden: bfloat16 [16, 1024, 4096], P('dp', 'ctx'), may hold values from -6 to 6
- queries: bfloat16 [16, 1024, 4096], P('dp', 'ctx'), may hold values from -6 to 6
- keys: bfloat16 [16, 1024, 256], P('dp', 'ctx'), may hold values from -6 to 6
- values: bfloat16 [16, 1024, 256], P('dp', 'ctx'), may hold values from -24 to 24
- out_weight: bfloat16 [4096, 4096], P(None, 'ctx'), may hold values from -0.09375 to 0.09375
- norm_gain: float32 [4096], replicated, may hold values from 0.1 to 1.9
- routes: int32 [16, 1024, 8], P('dp', 'ctx'), may hold values from 0 to 127, all different within a row; in each aligned block of 128 rows (0 to 127, 128 to 255, ..., all dimensions but the last counted through in order) at most 9 rows name the same one
- slot_scores: float32 [16, 1024, 8], P('dp', 'ctx'), may hold values from 0.1 to 1
- gate_weight: bfloat16 [128, 4096, 768], P(('dp', 'ctx')), may hold values from -0.09375 to 0.09375
- up_weight: bfloat16 [128, 4096, 768], P(('dp', 'ctx')), may hold values from -0.09375 to 0.09375
- down_weight: bfloat16 [128, 768, 4096], P(('dp', 'ctx')), may hold values from -0.21875 to 0.21875
Outputs:
- output: bfloat16 [16, 1024, 4096], P('dp', 'ctx')
The draws below stay inside these ranges and needn't reach their ends.
Inputs may be any that keep to these rules, and one draw needn't show every extreme that they name: In each aligned block of 128 tokens (the tokens of one device, sequences in order) no expert is named by more than 9 of the block's routes, a bound that some block reaches.
All inputs are finite; a program needn't handle non-finite values.
Results may differ from the reference program's by a relative error of at most 0.0065.
Values may be sent and summed in bfloat16 or wider, within the bound.
No kernel may reach another device: no remote copies, remote signals or barrier semaphores. Data moves between devices by JAX's collectives and lax.ppermute only.
A program may use at most 192 MiB of HBM per device.

```python
import math
import jax
import jax.numpy as jnp
import numpy as np
from jax import lax

D = 4096
HQ = 32
KVH = 2
DH = 128
HID = 768
TOP = 8
TOK_DEV = 128
SEQ = 1024
SEQS = 16
EXPERTS = 128
CAP = 9
N_DP = 16
N_CTX = 8


def draw_queries(key, part):
    sample_key = jax.random.fold_in(key, 3)
    sample = jnp.clip(jax.random.normal(sample_key, (SEQS, SEQ, HQ * DH), jnp.float32), -6.0, 6.0)
    return sample.astype(jnp.bfloat16)


def draw_keys(key, part):
    sample_key = jax.random.fold_in(key, 5)
    sample = jnp.clip(jax.random.normal(sample_key, (SEQS, SEQ, KVH * DH), jnp.float32), -6.0, 6.0)
    return sample.astype(jnp.bfloat16)


def block_scale(rng, dims, split, smallest, high):
    def one(dim, parts):
        steps = jax.random.uniform(jax.random.fold_in(jax.random.fold_in(rng, 6), dim), (parts,), jnp.float32, smallest / len(split), high / len(split))
        return jnp.repeat(jnp.exp(steps), dims[dim] // parts).reshape((-1,) + (1,) * (len(dims) - dim - 1))

    gain = one(*split[0])
    for cut in split[1:]:
        gain = gain * one(*cut)
    return gain


def routed_block(stream_key, own, number, rows, count, top, bound, lean):
    ranking = jax.random.permutation(stream_key, count)
    heavy_load, common = portions_of(count, rows * top, bound, lean, True), portions_of(count, rows * top, bound, lean, False)
    places = jnp.arange(count)

    def named(lengths, rotation):
        used = int((lengths > 0).sum())
        fixed = max(1, used // 4)
        moved = fixed + (places - fixed + rotation * (used - fixed)) % max(1, count - fixed)
        return jnp.zeros((count,), jnp.int32).at[ranking[jnp.where(places < fixed, places, moved)]].set(jnp.asarray(lengths, jnp.int32))

    lengths = jnp.where(number % 4 == 0, named(heavy_load, number // 4), named(common, number - number // 4 - 1))
    mixed = jax.random.permutation(jax.random.fold_in(own, 3), count)
    donor, taker = mixed[0:count // 2 * 2:2], mixed[1:count // 2 * 2:2]
    room = jnp.minimum(lengths[donor] - 1, bound - lengths[taker]) // 2
    room = jnp.where((donor == ranking[0]) | (taker == ranking[0]) | (lengths[taker] == 0), 0, jnp.maximum(room, 0))
    moved = jax.random.randint(jax.random.fold_in(own, 4), (count // 2,), 0, 1 << 20) % (room + 1)
    lengths = lengths.at[donor].add(-moved).at[taker].add(moved)
    labels = jnp.searchsorted(jnp.cumsum(lengths), jnp.arange(rows * top), side="right").astype(jnp.int32)
    grid = labels.reshape(top, rows).T
    grid = grid[jax.random.permutation(jax.random.fold_in(own, 1), rows)]
    rotation = jax.random.randint(jax.random.fold_in(own, 2), (rows, 1), 0, top)
    return jnp.take_along_axis(grid, (jnp.arange(top)[None, :] + rotation) % top, axis=1)


def portions_of(count, total, reach, skew, full):
    loads = [(1 << 20) // math.isqrt(grade ** skew) + 1 for grade in range(1, count + 1)]
    largest = reach if full else min(reach, max(-(-total // count), total * loads[0] // sum(loads)))
    least = 1 if total - largest >= count - 1 else 0
    counts, rest = [largest] + [least] * (count - 1), total - largest - least * (count - 1)
    while rest > 0:
        candidates = [i for i in range(1, count) if counts[i] < largest] or [i for i in range(1, count) if counts[i] < reach]
        whole, budget = sum([loads[i] for i in candidates]), rest
        for i in candidates:
            extra = min(reach - counts[i], max(1, budget * loads[i] // whole), rest)
            counts[i] = counts[i] + extra
            rest = rest - extra
    return np.array(counts)


def bell_draw(stream_key, dims, spread, reach, shards=(), held_as=jnp.bfloat16):
    values = jax.random.normal(stream_key, dims, jnp.float32) * spread
    if len(shards) > 0:
        values = block_scale(stream_key, dims, shards, -0.22, 0.18) * values
    return jnp.clip(values, min=-reach, max=reach).astype(held_as)


def setup_inputs(seed: int = 0) -> dict:
    key_list = jax.random.split(jax.random.key(seed), 12)
    hidden = bell_draw(key_list[0], (SEQS, SEQ, D), 1.0, 6.0, ((0, 16), (1, 8)))
    queries = draw_queries(jax.random.fold_in(key_list[11], 71), 0)
    keys = draw_keys(jax.random.fold_in(key_list[11], 71), 0)
    values = bell_draw(key_list[3], (SEQS, SEQ, KVH * DH), 4.0, 24.0, ((0, 16), (1, 8)))
    out_weight = bell_draw(key_list[4], (HQ * DH, D), (HQ * DH) ** -0.5, 0.09375, ((1, 8),))
    norm_gain = jnp.clip(1.0 + 0.18 * jax.random.normal(key_list[5], (D,), jnp.float32), 0.1, 1.9)
    routes_keys = jax.random.split(jax.random.fold_in(key_list[6], 1), SEQS * SEQ // TOK_DEV)
    routes_turns = jax.random.permutation(jax.random.fold_in(key_list[6], 3), SEQS * SEQ // TOK_DEV)
    routes = jax.vmap(lambda own, number: routed_block(jax.random.fold_in(key_list[6], 2), own, number, TOK_DEV, EXPERTS, TOP, CAP, 2))(routes_keys, routes_turns).reshape((SEQS, SEQ, TOP))
    slot_scores = jnp.clip(jnp.exp(math.log(1.0) - 2.3025851 * jax.random.uniform(key_list[7], (SEQS, SEQ, TOP), jnp.float32) ** block_scale(key_list[7], (SEQS, SEQ, TOP), ((0, 16), (1, 8)), -0.2, 0.2)), 0.1, 1.0)
    gate_weight = bell_draw(key_list[8], (EXPERTS, D, HID), D ** -0.5, 0.09375, ((0, 128),))
    up_weight = bell_draw(key_list[9], (EXPERTS, D, HID), D ** -0.5, 0.09375, ((0, 128),))
    down_weight = bell_draw(key_list[10], (EXPERTS, HID, D), HID ** -0.5, 0.21875, ((0, 128),))
    return {"hidden": hidden, "queries": queries, "keys": keys, "values": values, "out_weight": out_weight, "norm_gain": norm_gain, "routes": routes, "slot_scores": slot_scores, "gate_weight": gate_weight, "up_weight": up_weight, "down_weight": down_weight}


def expert_ffn(inputs, w_gate, w_up, w_down):
    gated = jnp.dot(inputs, w_gate, preferred_element_type=jnp.float32)
    lifted = jnp.dot(inputs, w_up, preferred_element_type=jnp.float32)
    activated = (jax.nn.silu(gated) * lifted).astype(jnp.bfloat16)
    return jnp.dot(activated, w_down, preferred_element_type=jnp.float32).astype(jnp.bfloat16)

def attend(triple):
    query_rows, key_rows, value_rows = triple
    group_size = HQ // KVH
    length = query_rows.shape[0]
    query_four = query_rows.reshape(length, KVH, group_size, DH).astype(jnp.float32)
    key_three = key_rows.reshape(length, KVH, DH).astype(jnp.float32)
    value_three = value_rows.reshape(length, KVH, DH).astype(jnp.float32)
    scores = jnp.einsum('qkgd,jkd->kgqj', query_four, key_three) * DH ** (-0.5)
    position = jnp.arange(length)
    causal = position[None, :] <= position[:, None]
    scores = jnp.where(causal, scores, -1e+30)
    row_max = lax.optimization_barrier(jnp.max(scores, axis=-1, keepdims=True))
    weights = jnp.where(causal, jnp.exp(scores - row_max), 0.0)
    total_weight = lax.optimization_barrier(jnp.sum(weights, axis=-1))
    rounded = lax.optimization_barrier(weights.astype(jnp.bfloat16)).astype(jnp.float32)
    numerator = jnp.einsum('kgqj,jkd->kgqd', rounded, value_three)
    attended = numerator / total_weight[..., None]
    return jnp.transpose(attended, (2, 0, 1, 3)).reshape(length, HQ * DH).astype(jnp.bfloat16)

def block_ranks(block_ids):
    one_hot = (block_ids[:, None] == jnp.arange(EXPERTS)[None, :]).astype(jnp.int32)
    earlier = jnp.cumsum(one_hot, axis=0) - one_hot
    return lax.optimization_barrier(jnp.sum(earlier * one_hot, axis=1)).astype(jnp.int32)

def reference(hidden, queries, keys, values, out_weight, norm_gain, routes, slot_scores, gate_weight, up_weight, down_weight):
    tokens_all = SEQS * SEQ
    attended = lax.map(attend, (queries, keys, values))
    projected = jnp.dot(attended.reshape(tokens_all, HQ * DH), out_weight, preferred_element_type=jnp.float32).astype(jnp.bfloat16)
    residual = hidden.reshape(tokens_all, D).astype(jnp.float32) + projected.astype(jnp.float32)
    normed = (residual * lax.rsqrt(lax.optimization_barrier(jnp.mean(residual * residual, axis=1, keepdims=True)) + 1e-06) * norm_gain).astype(jnp.bfloat16)
    scores_flat = slot_scores.reshape(tokens_all, TOP)
    slot_gates = scores_flat / lax.optimization_barrier(jnp.sum(scores_flat, axis=1, keepdims=True))
    flat_gates = slot_gates.reshape(tokens_all * TOP)
    blocks = N_DP * N_CTX
    expert_of = routes.reshape(blocks, TOK_DEV * TOP).astype(jnp.int32)
    ranks = lax.map(block_ranks, expert_of)
    block_of = jnp.broadcast_to(jnp.arange(blocks, dtype=jnp.int32)[:, None], (blocks, TOK_DEV * TOP))
    row_in = block_of * CAP + ranks
    entry = jnp.arange(tokens_all * TOP, dtype=jnp.int32).reshape(blocks, TOK_DEV * TOP)
    table = jnp.full((EXPERTS, blocks * CAP), tokens_all * TOP, jnp.int32)
    table = table.at[expert_of.reshape(-1), row_in.reshape(-1)].set(entry.reshape(-1))

    def per_expert(combined, inputs):
        table_row, w_gate, w_up, w_down = inputs
        filled = table_row < tokens_all * TOP
        safe = jnp.where(filled, table_row, 0).astype(jnp.int32)
        token_index = (safe // TOP).astype(jnp.int32)
        expert_out = expert_ffn(normed[token_index], w_gate, w_up, w_down)
        weight = jnp.where(filled, flat_gates[safe], 0.0)
        combined = combined.at[token_index].add(weight[:, None] * expert_out.astype(jnp.float32))
        return (combined, None)
    combined, _ = lax.scan(per_expert, jnp.zeros((tokens_all, D), jnp.float32), (table, gate_weight, up_weight, down_weight))
    return (residual + combined).astype(jnp.bfloat16).reshape(SEQS, SEQ, D)
```

```python
import jax
import jax.numpy as jnp
from jax import lax
from jax.sharding import Mesh, PartitionSpec as P

HQ = 32
KVH = 2
DH = 128
TOP = 8
EXPERTS = 128
FULL = 8
CHUNKS = 2

DP = ("z", "xl", "core")
CTX = ("xh", "y")
ALL = DP + CTX
BF = jnp.bfloat16
F32 = jnp.float32


def exchange(blocks, axes):
    return lax.all_to_all(blocks, axes, split_axis=0, concat_axis=0, tiled=True)


def neighbour_pairs():
    pairs = []
    for z in range(4):
        for xl in range(2):
            for core in range(2):
                for xh in range(2):
                    for y in range(4):
                        src = (((z * 2 + xl) * 2 + core) * 2 + xh) * 4 + y
                        dst = (((z * 2 + 1 - xl) * 2 + core) * 2 + 1 - xh) * 4 + y
                        pairs.append((src, dst))
    return pairs


def shift(block, step):
    return lax.ppermute(block, "y", [(i, (i + step) % 4) for i in range(4)])


def partner_weight(out_weight):
    core = lax.axis_index("core")
    half = out_weight.shape[0] // 2
    mine = lax.dynamic_slice_in_dim(out_weight, core * half, half, axis=0)
    fetched = lax.ppermute(mine, ALL, neighbour_pairs())
    other = lax.ppermute(fetched, "core", [(0, 1), (1, 0)])
    first = jnp.where(core == 0, fetched, other)
    second = jnp.where(core == 0, other, fetched)
    return jnp.concatenate([first, second], axis=0)


def attention(queries, keys, values):
    tok_count = queries.shape[0]
    group_size = HQ // KVH
    ctx_index = lax.axis_index(CTX)
    query_rows = queries.reshape(tok_count, KVH, group_size, DH)
    query_pos = ctx_index * tok_count + jnp.arange(tok_count, dtype=jnp.int32)
    pair = jnp.concatenate([keys, values], axis=1)
    width = keys.shape[1]
    gathered = exchange(jnp.broadcast_to(pair[None], (8,) + pair.shape), CTX)
    gathered = gathered.reshape(8 * tok_count, 2 * width)
    key_count = gathered.shape[0]
    key_rows = gathered[:, :width].reshape(key_count, KVH, DH)
    value_rows = gathered[:, width:].reshape(key_count, KVH, DH)
    key_pos = jnp.arange(key_count, dtype=jnp.int32)
    scores = (
        jnp.einsum("qkgd,jkd->kgqj", query_rows, key_rows, preferred_element_type=F32)
        * DH ** (-0.5)
    )
    causal = key_pos[None, :] <= query_pos[:, None]
    scores = jnp.where(causal, scores, -1e30)
    row_max = jnp.max(scores, axis=-1, keepdims=True)
    weights = jnp.where(causal, jnp.exp(scores - row_max), 0.0)
    total = jnp.sum(weights, axis=-1)
    numerator = jnp.einsum(
        "kgqj,jkd->kgqd", weights.astype(BF), value_rows, preferred_element_type=F32
    )
    attended = numerator / total[..., None]
    return jnp.transpose(attended, (2, 0, 1, 3)).reshape(tok_count, HQ * DH).astype(BF)


def project(attended, out_weight):
    partner = partner_weight(out_weight)
    width = attended.shape[1]

    def columns(rows):
        own = jnp.dot(rows, out_weight, preferred_element_type=F32).astype(BF)
        pair = jnp.dot(rows, partner, preferred_element_type=F32).astype(BF)
        return jnp.concatenate([own, pair], axis=1)

    below = shift(attended, 1)
    above = shift(attended, -1)
    far_left = shift(below[:, : width // 2], 1)
    far_right = shift(above[:, width // 2 :], -1)
    here = columns(attended)
    from_above = shift(columns(below), -1)
    from_below = shift(columns(above), 1)
    from_far = shift(columns(jnp.concatenate([far_left, far_right], axis=1)), 2)
    tok = attended.shape[0]
    y = lax.axis_index("y")
    xh = lax.axis_index("xh")
    ring = jnp.stack([here, from_above * 1, from_far, from_below])
    own_first = ring.reshape(4, tok, 2, 512).transpose(2, 0, 1, 3)
    turned = lax.dynamic_slice_in_dim(
        jnp.concatenate([own_first, own_first], axis=1), (4 - y) % 4, 4, axis=1
    )
    turned = jnp.where(xh == 0, turned, turned[::-1])
    return turned.reshape(8, tok, 512).transpose(1, 0, 2).reshape(tok, width)


def slots_of(routes, slot_gates):
    tok = routes.shape[0]
    named = routes[:, :, None] == jnp.arange(EXPERTS, dtype=jnp.int32)[None, None, :]
    hit = jnp.any(named, axis=1)
    gate = jnp.sum(jnp.where(named, slot_gates[:, :, None], 0.0), axis=1)
    before = jnp.arange(tok)[None, :] < jnp.arange(tok)[:, None]
    rank = jnp.dot(before.astype(BF), hit.astype(BF), preferred_element_type=F32)
    return hit, jnp.where(hit, rank, -1.0), gate


def local(
    hidden,
    queries,
    keys,
    values,
    out_weight,
    norm_gain,
    routes,
    slot_scores,
    gate_weight,
    up_weight,
    down_weight,
):
    tok, width = hidden.shape[1:]
    attended = attention(queries[0], keys[0], values[0])

    score_rows = slot_scores[0]
    slot_gates = score_rows / jnp.sum(score_rows, axis=1, keepdims=True)
    hit, rank, gate = slots_of(routes[0], slot_gates)
    places = jnp.arange(FULL, dtype=F32)
    pick = (rank.T[:, None, :] == places[None, :, None]).astype(BF).reshape(EXPERTS * FULL, tok)
    pick_last = (rank.T == float(FULL)).astype(BF)
    weigh = jnp.where(rank[:, :, None] == places, gate[:, :, None], 0.0).reshape(tok, EXPERTS * FULL)
    weigh_last = jnp.where(rank == float(FULL), gate, 0.0)
    weigh = jnp.concatenate([weigh, weigh_last], axis=1)
    high = weigh.astype(BF)
    low = (weigh - high.astype(F32)).astype(BF)
    split = jnp.concatenate([high, low], axis=0)

    projected = project(attended, out_weight)
    residual = hidden[0].astype(F32) + projected.astype(F32)
    normed = (
        residual
        * lax.rsqrt(jnp.mean(residual * residual, axis=1, keepdims=True) + 1e-06)
        * norm_gain
    ).astype(BF)

    step = width // CHUNKS
    w_gate, w_up, w_down = gate_weight[0], up_weight[0], down_weight[0]
    last = jnp.dot(pick_last, normed, preferred_element_type=F32).astype(BF)
    last = exchange(last.reshape(EXPERTS, 8, width // 8), ALL).reshape(EXPERTS, width)
    gated = lifted = 0.0
    for c in range(CHUNKS):
        cols = slice(c * step, (c + 1) * step)
        sent = jnp.dot(pick, normed[:, cols], preferred_element_type=F32).astype(BF)
        got = exchange(sent.reshape(EXPERTS, FULL, step), ALL).reshape(EXPERTS * FULL, step)
        got = jnp.concatenate([got, last[:, cols]], axis=0)
        gated = gated + jnp.dot(got, w_gate[cols], preferred_element_type=F32)
        lifted = lifted + jnp.dot(got, w_up[cols], preferred_element_type=F32)
    activated = (jax.nn.silu(gated) * lifted).astype(BF)

    rows = EXPERTS * FULL
    back_last = jnp.dot(activated[rows:], w_down, preferred_element_type=F32).astype(BF)
    back_last = exchange(back_last.reshape(EXPERTS, 8, width // 8), ALL).reshape(EXPERTS, width)
    outs = []
    for c in range(CHUNKS):
        cols = slice(c * step, (c + 1) * step)
        served = jnp.dot(activated[:rows], w_down[:, cols], preferred_element_type=F32).astype(BF)
        back = exchange(served.reshape(EXPERTS, FULL, step), ALL).reshape(rows, step)
        back = jnp.concatenate([back, back_last[:, cols]], axis=0)
        sums = jnp.dot(split, back, preferred_element_type=F32)
        outs.append((residual[:, cols] + (sums[:tok] + sums[tok:])).astype(BF))
    return jnp.concatenate(outs, axis=1)[None]


def solution(mesh):
    fine = Mesh(mesh.devices.reshape(4, 2, 2, 2, 4), ALL)
    return jax.shard_map(
        local,
        mesh=fine,
        in_specs=(
            P(DP, CTX, None),
            P(DP, CTX, None),
            P(DP, CTX, None),
            P(DP, CTX, None),
            P(None, CTX),
            P(),
            P(DP, CTX, None),
            P(DP, CTX, None),
            P(ALL, None, None),
            P(ALL, None, None),
            P(ALL, None, None),
        ),
        out_specs=P(DP, CTX, None),
        check_vma=False,
    )
```

```python
import jax
import jax.numpy as jnp
from jax import lax
from jax.experimental import pallas as pl
from jax.experimental.pallas import tpu as pltpu
from jax.sharding import Mesh, PartitionSpec as P


HQ = 32
KVH = 2
DH = 128
EXPERTS = 128
FULL = 8
SLOTS = EXPERTS * FULL
WIDTH = 4096
PACK = WIDTH // 8
OUT_FIRST = 3072
BACK_FIRST = 1024
TILE = 256

DP = ("z", "xl", "core")
CTX = ("xh", "y")
ALL = DP + CTX
BF = jnp.bfloat16
F32 = jnp.float32


def exchange(blocks, axes):
    return lax.all_to_all(blocks, axes, split_axis=0, concat_axis=0, tiled=True)


def neighbour_pairs():
    pairs = []
    for z in range(4):
        for xl in range(2):
            for core in range(2):
                for xh in range(2):
                    for y in range(4):
                        src = (((z * 2 + xl) * 2 + core) * 2 + xh) * 4 + y
                        dst = (((z * 2 + 1 - xl) * 2 + core) * 2 + 1 - xh) * 4 + y
                        pairs.append((src, dst))
    return pairs


def shift(block, step):
    return lax.ppermute(block, "y", [(i, (i + step) % 4) for i in range(4)])


def attention(queries, keys, values):
    tok_count = queries.shape[0]
    group_size = HQ // KVH
    ctx_index = lax.axis_index(CTX)
    query_rows = queries.reshape(tok_count, KVH, group_size, DH)
    query_pos = ctx_index * tok_count + jnp.arange(tok_count, dtype=jnp.int32)
    pair = jnp.concatenate([keys, values], axis=1)
    width = keys.shape[1]
    gathered = exchange(jnp.broadcast_to(pair[None], (8,) + pair.shape), CTX)
    gathered = gathered.reshape(8 * tok_count, 2 * width)
    key_count = gathered.shape[0]
    key_pos = jnp.arange(key_count, dtype=jnp.int32)
    causal = key_pos[None, :] <= query_pos[:, None]
    outs = []
    for head in range(KVH):
        key_rows = gathered[:, head * DH : (head + 1) * DH]
        value_rows = gathered[:, width + head * DH : width + (head + 1) * DH]
        scores = (
            jnp.einsum("qgd,jd->gqj", query_rows[:, head], key_rows, preferred_element_type=F32)
            * DH ** (-0.5)
        )
        scores = jnp.where(causal, scores, -1e30)
        row_max = jnp.max(scores, axis=-1, keepdims=True)
        weights = jnp.where(causal, jnp.exp(scores - row_max), 0.0)
        total = jnp.sum(weights, axis=-1)
        numerator = jnp.einsum(
            "gqj,jd->gqd", weights.astype(BF), value_rows, preferred_element_type=F32
        )
        attended = numerator / total[..., None]
        outs.append(jnp.transpose(attended, (1, 0, 2)).reshape(tok_count, group_size * DH).astype(BF))
    return outs


def project(attended, out_weight):
    first, second = attended
    tok, half = first.shape
    core = lax.axis_index("core")
    mine = lax.dynamic_slice_in_dim(out_weight, core * half, half, axis=0)
    fetched = lax.ppermute(mine, ALL, neighbour_pairs())
    below_a, above_a = shift(first, 1), shift(first, -1)
    below_b, above_b = shift(second, 1), shift(second, -1)
    far_a = shift(below_a, 1)
    far_b = shift(above_b, -1)
    other = lax.ppermute(fetched, "core", [(0, 1), (1, 0)])
    partner_a = jnp.where(core == 0, fetched, other)
    partner_b = jnp.where(core == 0, other, fetched)

    def columns(rows_a, rows_b):
        def product(top, bottom):
            return (
                jnp.dot(rows_a, top, preferred_element_type=F32)
                + jnp.dot(rows_b, bottom, preferred_element_type=F32)
            ).astype(BF)

        own = product(out_weight[:half], out_weight[half:])
        return jnp.concatenate([own, product(partner_a, partner_b)], axis=1)

    here = columns(first, second)
    from_above = shift(columns(below_a, below_b), -1)
    from_below = shift(columns(above_a, above_b), 1)
    from_far = shift(columns(far_a, far_b), 2)
    y = lax.axis_index("y")
    xh = lax.axis_index("xh")
    ring = jnp.stack([here, from_above, from_far, from_below])
    own_first = ring.reshape(4, tok, 2, 512).transpose(2, 0, 1, 3)
    turned = lax.dynamic_slice_in_dim(
        jnp.concatenate([own_first, own_first], axis=1), (4 - y) % 4, 4, axis=1
    )
    turned = jnp.where(xh == 0, turned, turned[::-1])
    return turned.reshape(8, tok, 512).transpose(1, 0, 2).reshape(tok, 2 * half)


def product(left, right):
    return jnp.dot(left, right, preferred_element_type=F32)


def shuffle(packing):
    by_row = lax.broadcasted_iota(jnp.int32, (128, 128), 0 if packing else 1)
    by_piece = lax.broadcasted_iota(jnp.int32, (128, 128), 1 if packing else 0)
    return (lax.rem(by_row, 8) * 16 + lax.div(by_row, 8) == by_piece).astype(F32).astype(BF)


def pack(rows, out_ref, start):
    order = shuffle(True)
    for i in range(EXPERTS // 16):
        pieces = [rows[16 * i : 16 * i + 16, PACK * s : PACK * (s + 1)] for s in range(8)]
        packed = product(order, jnp.concatenate(pieces, axis=0))
        out_ref[128 * i : 128 * (i + 1), start : start + PACK] = packed.astype(BF)


def unpack(in_ref, start, rows):
    order = shuffle(False)
    for i in range(EXPERTS // 16):
        packed = in_ref[128 * i : 128 * (i + 1), start : start + PACK]
        pieces = product(order, packed).astype(BF)
        for s in range(8):
            rows[16 * i : 16 * i + 16, PACK * s : PACK * (s + 1)] = pieces[16 * s : 16 * s + 16]


def tiles(count, body):
    def step(i, carry):
        body(pl.ds(pl.multiple_of(i * TILE, TILE), TILE))
        return carry

    lax.fori_loop(0, count // TILE, step, 0)


def make_kernel(normed_ref, pick_ref, last_ref, out_ref, rows):
    rows[...] = product(last_ref[...], normed_ref[...]).astype(BF)
    pack(rows, out_ref, OUT_FIRST)

    def body(at):
        out_ref[at, :OUT_FIRST] = product(pick_ref[at], normed_ref[:, :OUT_FIRST]).astype(BF)

    tiles(SLOTS, body)


def silu_product(gated, lifted):
    return (gated / (1.0 + jnp.exp(-gated)) * lifted).astype(BF)


def first_kernel(got_ref, gate_ref, up_ref, down_ref, gated_ref, lifted_ref, last_ref, rows):
    def body(at):
        x = got_ref[at, :OUT_FIRST]
        gated_ref[at] = product(x, gate_ref[:OUT_FIRST])
        lifted_ref[at] = product(x, up_ref[:OUT_FIRST])

    tiles(SLOTS, body)
    unpack(got_ref, OUT_FIRST, rows)
    x = rows[...]
    activated = silu_product(product(x, gate_ref[...]), product(x, up_ref[...]))
    rows[...] = product(activated, down_ref[...]).astype(BF)
    pack(rows, last_ref, 0)


def second_kernel(got_ref, gate_ref, up_ref, down_ref, gated_ref, lifted_ref, last_ref, act_ref, out_ref):
    def body(at):
        x = got_ref[at]
        gated = gated_ref[at] + product(x, gate_ref[...])
        lifted = lifted_ref[at] + product(x, up_ref[...])
        activated = silu_product(gated, lifted)
        act_ref[at] = activated
        out_ref[at, :BACK_FIRST] = product(activated, down_ref[...]).astype(BF)
        out_ref[at, BACK_FIRST:] = last_ref[at]

    tiles(SLOTS, body)


def finish_kernel(base_ref, split_ref, back_ref, out_ref):
    fixed = BACK_FIRST // PACK

    @pl.when(pl.program_id(0) < fixed)
    def _():
        out_ref[...] = base_ref[...].astype(BF)

    @pl.when(pl.program_id(0) >= fixed)
    def _():
        sums = product(split_ref[...], back_ref[...])
        tok = base_ref.shape[0]
        out_ref[...] = (base_ref[...] + (sums[:tok] + sums[tok:])).astype(BF)


def whole(shape, index=(0, 0)):
    return pl.BlockSpec(shape, lambda i: index)


def call(body, grid, in_specs, out_specs, out_shape, scratch=(), flops=0, moved=0):
    return pl.pallas_call(
        body,
        grid=grid,
        in_specs=in_specs,
        out_specs=out_specs,
        out_shape=out_shape,
        scratch_shapes=scratch,
        compiler_params=pltpu.CompilerParams(vmem_limit_bytes=56 * 1024 * 1024),
        cost_estimate=pl.CostEstimate(flops=flops, bytes_accessed=moved, transcendentals=0),
    )


def two_terms(weigh):
    high = weigh.astype(BF)
    low = (weigh - high.astype(F32)).astype(BF)
    return jnp.concatenate([high, low], axis=0)


def slots_of(routes, slot_gates):
    tok = routes.shape[0]
    named = routes[:, :, None] == jnp.arange(EXPERTS, dtype=jnp.int32)[None, None, :]
    hit = jnp.any(named, axis=1)
    gate = jnp.sum(jnp.where(named, slot_gates[:, :, None], 0.0), axis=1)
    before = jnp.arange(tok)[None, :] < jnp.arange(tok)[:, None]
    rank = jnp.dot(before.astype(BF), hit.astype(BF), preferred_element_type=F32)
    return hit, jnp.where(hit, rank, -1.0), gate


def layer(
    hidden,
    queries,
    keys,
    values,
    out_weight,
    norm_gain,
    routes,
    slot_scores,
    gate_weight,
    up_weight,
    down_weight,
):
    tok, _ = hidden.shape[1:]
    attended = attention(queries[0], keys[0], values[0])

    score_rows = slot_scores[0]
    slot_gates = score_rows / jnp.sum(score_rows, axis=1, keepdims=True)
    _, rank, gate = slots_of(routes[0], slot_gates)
    places = jnp.arange(FULL, dtype=F32)
    pick = (rank.T[:, None, :] == places[None, :, None]).astype(BF).reshape(EXPERTS * FULL, tok)
    pick_last = (rank.T == float(FULL)).astype(BF)
    weigh = jnp.where(rank[:, :, None] == places, gate[:, :, None], 0.0).reshape(tok, EXPERTS * FULL)
    weigh_last = jnp.where(rank == float(FULL), gate, 0.0)
    split, split_last = two_terms(weigh), two_terms(weigh_last)

    projected = project(attended, out_weight)
    residual = hidden[0].astype(F32) + projected.astype(F32)
    normed = (
        residual
        * lax.rsqrt(jnp.mean(residual * residual, axis=1, keepdims=True) + 1e-06)
        * norm_gain
    ).astype(BF)

    hid = gate_weight.shape[2]
    w_gate, w_up, w_down = gate_weight[0], up_weight[0], down_weight[0]
    shape = jax.ShapeDtypeStruct
    rest = WIDTH - OUT_FIRST
    send_first = OUT_FIRST + PACK
    back_first = BACK_FIRST + PACK
    nine = pltpu.VMEM((EXPERTS, WIDTH), BF)

    sent = call(
        make_kernel, (1,),
        [whole((tok, WIDTH)), whole((SLOTS, tok)), whole((EXPERTS, tok))],
        whole((SLOTS, send_first)), shape((SLOTS, send_first), BF), [nine],
        flops=2 * SLOTS * tok * send_first, moved=SLOTS * send_first * 2,
    )(normed, pick, pick_last)
    got = exchange(sent.reshape(EXPERTS, FULL, send_first), ALL).reshape(SLOTS, send_first)
    sent_rest = product(pick, normed[:, OUT_FIRST:]).astype(BF)
    got_rest = exchange(sent_rest.reshape(EXPERTS, FULL, rest), ALL).reshape(SLOTS, rest)
    gated, lifted, last = call(
        first_kernel, (1,),
        [whole((SLOTS, send_first)), whole((WIDTH, hid)), whole((WIDTH, hid)), whole((hid, WIDTH))],
        [whole((SLOTS, hid)), whole((SLOTS, hid)), whole((SLOTS, PACK))],
        [shape((SLOTS, hid), F32), shape((SLOTS, hid), F32), shape((SLOTS, PACK), BF)], [nine],
        flops=4 * SLOTS * OUT_FIRST * hid, moved=SLOTS * (send_first + 4 * hid) * 2 + WIDTH * hid * 6,
    )(got, w_gate, w_up, w_down)
    activated, served = call(
        second_kernel, (1,),
        [
            whole((SLOTS, rest)), whole((rest, hid), (OUT_FIRST // rest, 0)),
            whole((rest, hid), (OUT_FIRST // rest, 0)), whole((hid, BACK_FIRST)),
            whole((SLOTS, hid)), whole((SLOTS, hid)), whole((SLOTS, PACK)),
        ],
        [whole((SLOTS, hid)), whole((SLOTS, back_first))],
        [shape((SLOTS, hid), BF), shape((SLOTS, back_first), BF)],
        flops=6 * SLOTS * rest * hid, moved=SLOTS * (rest + back_first + 4 * hid) * 2 + rest * hid * 6,
    )(got_rest, w_gate, w_up, w_down, gated, lifted, last)
    back = exchange(served.reshape(EXPERTS, FULL, back_first), ALL).reshape(SLOTS, back_first)
    served_rest = product(activated, w_down[:, BACK_FIRST:]).astype(BF)
    back_rest = exchange(
        served_rest.reshape(EXPERTS, FULL, WIDTH - BACK_FIRST), ALL
    ).reshape(SLOTS, WIDTH - BACK_FIRST)

    sums = product(split, back[:, :BACK_FIRST])
    nines = product(split_last, back[:, BACK_FIRST:].reshape(EXPERTS, WIDTH))
    base = residual + (nines[:tok] + nines[tok:])
    base = jnp.concatenate(
        [base[:, :BACK_FIRST] + (sums[:tok] + sums[tok:]), base[:, BACK_FIRST:]], axis=1
    )
    fixed = BACK_FIRST // PACK
    out = call(
        finish_kernel, (WIDTH // PACK,),
        [
            pl.BlockSpec((tok, PACK), lambda i: (0, i)),
            whole((2 * tok, SLOTS)),
            pl.BlockSpec((SLOTS, PACK), lambda i: (0, jnp.maximum(i - fixed, 0))),
        ],
        pl.BlockSpec((tok, PACK), lambda i: (0, i)), shape((tok, WIDTH), BF),
        flops=4 * tok * SLOTS * WIDTH, moved=SLOTS * WIDTH * 2,
    )(base, split, back_rest)
    return out[None]


def solution(mesh):
    fine = Mesh(mesh.devices.reshape(4, 2, 2, 2, 4), ALL)
    return jax.shard_map(
        layer,
        mesh=fine,
        in_specs=(
            P(DP, CTX, None),
            P(DP, CTX, None),
            P(DP, CTX, None),
            P(DP, CTX, None),
            P(None, CTX),
            P(),
            P(DP, CTX, None),
            P(DP, CTX, None),
            P(ALL, None, None),
            P(ALL, None, None),
            P(ALL, None, None),
        ),
        out_specs=P(DP, CTX, None),
        check_vma=False,
    )
```

```python
import jax
import jax.numpy as jnp
from jax import lax
from jax.experimental import pallas as pl
from jax.experimental.pallas import tpu as pltpu
from jax.sharding import Mesh, PartitionSpec as P


KVH = 2
DH = 128
EXPERTS = 128
FULL = 8
SLOTS = EXPERTS * FULL
WIDTH = 4096
PACK = WIDTH // 8
OUT_FIRST = 3072
BACK_FIRST = 1024
TILE = 256
FINISH = 1024

DP = ("z", "xl", "core")
CTX = ("xh", "y")
ALL = DP + CTX
BF = jnp.bfloat16
F32 = jnp.float32


def exchange(blocks, axes):
    return lax.all_to_all(blocks, axes, split_axis=0, concat_axis=0, tiled=True)


def neighbour_pairs():
    pairs = []
    for z in range(4):
        for xl in range(2):
            for core in range(2):
                for xh in range(2):
                    for y in range(4):
                        src = (((z * 2 + xl) * 2 + core) * 2 + xh) * 4 + y
                        dst = (((z * 2 + 1 - xl) * 2 + core) * 2 + 1 - xh) * 4 + y
                        pairs.append((src, dst))
    return pairs


def shift(block, step):
    return lax.ppermute(block, "y", [(i, (i + step) % 4) for i in range(4)])


def gather_pair(keys, values):
    pair = jnp.concatenate([keys, values], axis=1)
    gathered = exchange(jnp.broadcast_to(pair[None], (8,) + pair.shape), CTX)
    return gathered.reshape(8 * pair.shape[0], pair.shape[1])


def attend_kernel(place_ref, query_ref, key_ref, value_ref, out_ref, bias):
    tok = query_ref.shape[0]
    heads = query_ref.shape[1] // DH

    @pl.when(pl.program_id(0) == 0)
    def _():
        query_pos = place_ref[0] * tok + lax.broadcasted_iota(jnp.int32, bias.shape, 0)
        key_pos = lax.broadcasted_iota(jnp.int32, bias.shape, 1)
        bias[...] = jnp.where(key_pos <= query_pos, 0.0, -1e30)

    for head in range(heads):
        at = slice(head * DH, (head + 1) * DH)
        scores = lax.dot_general(
            query_ref[:, at], key_ref[...], (((1,), (1,)), ((), ())), preferred_element_type=F32
        )
        scores = scores * DH ** (-0.5) + bias[...]
        weights = jnp.exp(scores - jnp.max(scores, axis=1, keepdims=True))
        total = jnp.sum(weights, axis=1, keepdims=True)
        out_ref[:, at] = (product(weights.astype(BF), value_ref[...]) / total).astype(BF)


def attend(place, queries, gathered, head):
    tok = queries.shape[0]
    keys = gathered.shape[0]
    half = queries.shape[1] // KVH
    block = 4 * DH
    steps = half // block
    return pl.pallas_call(
        attend_kernel,
        grid_spec=pltpu.PrefetchScalarGridSpec(
            num_scalar_prefetch=1,
            grid=(steps,),
            in_specs=[
                pl.BlockSpec((tok, block), lambda i, p: (0, head * steps + i)),
                pl.BlockSpec((keys, DH), lambda i, p: (0, head)),
                pl.BlockSpec((keys, DH), lambda i, p: (0, KVH + head)),
            ],
            out_specs=pl.BlockSpec((tok, block), lambda i, p: (0, i)),
            scratch_shapes=[pltpu.VMEM((tok, keys), F32)],
        ),
        out_shape=jax.ShapeDtypeStruct((tok, half), BF),
        cost_estimate=pl.CostEstimate(
            flops=4 * tok * half * keys, bytes_accessed=4 * tok * half, transcendentals=tok * half * 8
        ),
    )(place, queries, gathered, gathered)


def own_kernel(*refs):
    *row_refs, weight_ref, out_ref = refs
    half = row_refs[0].shape[1]
    left = jnp.concatenate([ref[...] for ref in row_refs[0::2]], axis=0)
    right = jnp.concatenate([ref[...] for ref in row_refs[1::2]], axis=0)
    out = product(left, weight_ref[:half]) + product(right, weight_ref[half:])
    out_ref[...] = out.astype(BF)


def pair_kernel(core_ref, *refs):
    *row_refs, fetched_ref, other_ref, out_ref = refs
    left = jnp.concatenate([ref[...] for ref in row_refs[0::2]], axis=0)
    right = jnp.concatenate([ref[...] for ref in row_refs[1::2]], axis=0)
    swap = core_ref[0] == 1
    out = product(jnp.where(swap, right, left), fetched_ref[...])
    out = out + product(jnp.where(swap, left, right), other_ref[...])
    out_ref[...] = out.astype(BF)


def columns(rows, weight, core=None):
    flat = [part for pair in rows for part in pair]
    tok, half = flat[0].shape
    wide = weight[0].shape[1]
    count = len(rows) * tok
    body = own_kernel if core is None else pair_kernel
    vmem = pl.BlockSpec(memory_space=pltpu.VMEM)
    scalars = [] if core is None else [core]
    return pl.pallas_call(
        body,
        in_specs=[pl.BlockSpec(memory_space=pltpu.SMEM)] * len(scalars) + [vmem] * (len(flat) + len(weight)),
        out_specs=vmem,
        out_shape=jax.ShapeDtypeStruct((count, wide), BF),
        compiler_params=pltpu.CompilerParams(vmem_limit_bytes=32 * 1024 * 1024),
        cost_estimate=pl.CostEstimate(
            flops=4 * count * half * wide, bytes_accessed=4 * half * wide + 4 * count * half, transcendentals=0
        ),
    )(*scalars, *flat, *weight)


def project(attended, out_weight):
    first, second = attended
    tok, half = first.shape
    core = lax.axis_index("core")
    mine = lax.dynamic_slice_in_dim(out_weight, core * half, half, axis=0)
    fetched = lax.ppermute(mine, ALL, neighbour_pairs())
    below_a, above_a = shift(first, 1), shift(first, -1)
    below_b, above_b = shift(second, 1), shift(second, -1)
    far_a = shift(below_a, 1)
    far_b = shift(above_b, -1)
    other = lax.ppermute(fetched, "core", [(0, 1), (1, 0)])
    near = [(first, second), (below_a, below_b), (above_a, above_b)]
    far = [(far_a, far_b)]
    which = core.reshape(1)
    near_own = columns(near, [out_weight])
    near_pair = columns(near, [fetched, other], which)
    near = jnp.concatenate([near_own, near_pair], axis=1)
    from_above = shift(near[tok : 2 * tok], -1)
    from_below = shift(near[2 * tok :], 1)
    far_own = columns(far, [out_weight])
    far_pair = columns(far, [fetched, other], which)
    from_far = shift(jnp.concatenate([far_own, far_pair], axis=1), 2)
    return [near[:tok], from_above, from_far, from_below]


def product(left, right):
    return jnp.dot(left, right, preferred_element_type=F32)


def shuffle(packing):
    by_row = lax.broadcasted_iota(jnp.int32, (128, 128), 0 if packing else 1)
    by_piece = lax.broadcasted_iota(jnp.int32, (128, 128), 1 if packing else 0)
    return (lax.rem(by_row, 8) * 16 + lax.div(by_row, 8) == by_piece).astype(F32).astype(BF)


def packed_rows(rows):
    pieces = [rows[:, PACK * s : PACK * (s + 1)] for s in range(8)]
    return product(shuffle(True), jnp.concatenate(pieces, axis=0)).astype(BF)


def unpack(packed, rows, start):
    pieces = product(shuffle(False), packed).astype(BF)
    for s in range(8):
        rows[pl.ds(start, 16), PACK * s : PACK * (s + 1)] = pieces[16 * s : 16 * s + 16]


def make_kernel(
    place_ref, here_ref, above_ref, far_ref, below_ref, hidden_ref, gain_ref, pick_ref, last_ref,
    out_ref, rest_ref, residual_ref, normed,
):
    step = pl.program_id(0)

    @pl.when(step == 0)
    def _():
        for ahead, ref in enumerate((here_ref, above_ref, far_ref, below_ref)):
            y = lax.rem(place_ref[2] + ahead, 4)
            for part in range(2):
                high = place_ref[1] if part == 0 else 1 - place_ref[1]
                at = pl.ds(pl.multiple_of((high * 4 + y) * PACK, PACK), PACK)
                projected = ref[:, part * PACK : (part + 1) * PACK].astype(F32)
                residual_ref[:, at] = hidden_ref[:, at].astype(F32) + projected
        residual = residual_ref[...]
        mean = jnp.mean(residual * residual, axis=1, keepdims=True)
        normed[...] = (residual * lax.rsqrt(mean + 1e-06) * gain_ref[...]).astype(BF)

    picked = pick_ref[...]
    out_ref[:, :OUT_FIRST] = product(picked, normed[:, :OUT_FIRST]).astype(BF)
    out_ref[:, OUT_FIRST:] = packed_rows(product(last_ref[...], normed[...]).astype(BF))

    @pl.when(step == 0)
    def _():
        rest_ref[...] = normed[:, OUT_FIRST:]


def silu_product(gated, lifted):
    return (gated / (1.0 + jnp.exp(-gated)) * lifted).astype(BF)


def first_kernel(got_ref, gate_ref, up_ref, down_ref, gated_ref, lifted_ref, last_ref, rows):
    step = pl.program_id(0)
    x = got_ref[:, :OUT_FIRST]
    gated_ref[...] = product(x, gate_ref[:OUT_FIRST])
    lifted_ref[...] = product(x, up_ref[:OUT_FIRST])
    for i in range(TILE // 128):
        start = pl.multiple_of(step * (TILE // 8) + 16 * i, 16)
        unpack(got_ref[128 * i : 128 * (i + 1), OUT_FIRST:], rows, start)

    @pl.when(step == pl.num_programs(0) - 1)
    def _():
        x = rows[...]
        activated = silu_product(product(x, gate_ref[...]), product(x, up_ref[...]))
        served = product(activated, down_ref[...]).astype(BF)
        for i in range(EXPERTS // 16):
            last_ref[128 * i : 128 * (i + 1)] = packed_rows(served[16 * i : 16 * (i + 1)])


def second_kernel(got_ref, gate_ref, up_ref, down_ref, gated_ref, lifted_ref, last_ref, act_ref, out_ref):
    x = got_ref[...]
    gated = gated_ref[...] + product(x, gate_ref[...])
    lifted = lifted_ref[...] + product(x, up_ref[...])
    activated = silu_product(gated, lifted)
    act_ref[...] = activated
    out_ref[:, :BACK_FIRST] = product(activated, down_ref[...]).astype(BF)
    out_ref[:, BACK_FIRST:] = last_ref[...]


def finish_kernel(base_ref, split_ref, back_ref, out_ref):
    fixed = BACK_FIRST // FINISH

    @pl.when(pl.program_id(0) < fixed)
    def _():
        out_ref[...] = base_ref[...].astype(BF)

    @pl.when(pl.program_id(0) >= fixed)
    def _():
        sums = product(split_ref[...], back_ref[...])
        tok = base_ref.shape[0]
        out_ref[...] = (base_ref[...] + (sums[:tok] + sums[tok:])).astype(BF)


def whole(shape, index=(0, 0)):
    return pl.BlockSpec(shape, lambda i: index)


def tiled(shape):
    return pl.BlockSpec(shape, lambda i: (i, 0))


def call(body, grid, in_specs, out_specs, out_shape, scratch=(), flops=0, moved=0):
    return pl.pallas_call(
        body,
        grid=grid,
        in_specs=in_specs,
        out_specs=out_specs,
        out_shape=out_shape,
        scratch_shapes=scratch,
        compiler_params=pltpu.CompilerParams(vmem_limit_bytes=56 * 1024 * 1024),
        cost_estimate=pl.CostEstimate(flops=flops, bytes_accessed=moved, transcendentals=0),
    )


def two_terms(weigh):
    high = weigh.astype(BF)
    low = (weigh - high.astype(F32)).astype(BF)
    return jnp.concatenate([high, low], axis=0)


def slots_of(routes, slot_gates):
    tok = routes.shape[0]
    named = routes[:, :, None] == jnp.arange(EXPERTS, dtype=jnp.int32)[None, None, :]
    hit = jnp.any(named, axis=1)
    gate = jnp.sum(jnp.where(named, slot_gates[:, :, None], 0.0), axis=1)
    before = jnp.arange(tok)[None, :] < jnp.arange(tok)[:, None]
    rank = jnp.dot(before.astype(BF), hit.astype(BF), preferred_element_type=F32)
    return hit, jnp.where(hit, rank, -1.0), gate


def layer(
    hidden,
    queries,
    keys,
    values,
    out_weight,
    norm_gain,
    routes,
    slot_scores,
    gate_weight,
    up_weight,
    down_weight,
):
    tok, _ = hidden.shape[1:]
    place = jnp.stack([lax.axis_index(CTX), lax.axis_index("xh"), lax.axis_index("y")])
    gathered = gather_pair(keys[0], values[0])
    first = attend(place, queries[0], gathered, 0)
    second = attend(place, queries[0], gathered, 1)

    score_rows = slot_scores[0]
    slot_gates = score_rows / jnp.sum(score_rows, axis=1, keepdims=True)
    _, rank, gate = slots_of(routes[0], slot_gates)
    places = jnp.arange(FULL, dtype=F32)
    pick = (rank.T[:, None, :] == places[None, :, None]).astype(BF).reshape(EXPERTS * FULL, tok)
    pick_last = (rank.T == float(FULL)).astype(BF)
    weigh = jnp.where(rank[:, :, None] == places, gate[:, :, None], 0.0).reshape(tok, EXPERTS * FULL)
    weigh_last = jnp.where(rank == float(FULL), gate, 0.0)
    split, split_last = two_terms(weigh), two_terms(weigh_last)

    columns_home = project((first, second), out_weight)

    hid = gate_weight.shape[2]
    w_gate, w_up, w_down = gate_weight[0], up_weight[0], down_weight[0]
    shape = jax.ShapeDtypeStruct
    rest = WIDTH - OUT_FIRST
    send_first = OUT_FIRST + PACK
    back_first = BACK_FIRST + PACK
    nine = pltpu.VMEM((EXPERTS, WIDTH), BF)

    sent, normed_rest, residual = pl.pallas_call(
        make_kernel,
        name="make",
        grid_spec=pltpu.PrefetchScalarGridSpec(
            num_scalar_prefetch=1,
            grid=(SLOTS // 128,),
            in_specs=[pl.BlockSpec((tok, 2 * PACK), lambda i, p: (0, 0))] * 4
            + [
                pl.BlockSpec((tok, WIDTH), lambda i, p: (0, 0)),
                pl.BlockSpec((1, WIDTH), lambda i, p: (0, 0)),
                pl.BlockSpec((128, tok), lambda i, p: (i, 0)),
                pl.BlockSpec((16, tok), lambda i, p: (i, 0)),
            ],
            out_specs=[
                pl.BlockSpec((128, send_first), lambda i, p: (i, 0)),
                pl.BlockSpec((tok, rest), lambda i, p: (0, 0)),
                pl.BlockSpec((tok, WIDTH), lambda i, p: (0, 0)),
            ],
            scratch_shapes=[pltpu.VMEM((tok, WIDTH), BF)],
        ),
        out_shape=[
            shape((SLOTS, send_first), BF), shape((tok, rest), BF), shape((tok, WIDTH), F32)
        ],
        compiler_params=pltpu.CompilerParams(vmem_limit_bytes=32 * 1024 * 1024),
        cost_estimate=pl.CostEstimate(
            flops=2 * SLOTS * tok * send_first, bytes_accessed=SLOTS * send_first * 2, transcendentals=0
        ),
    )(place, *columns_home, hidden[0], norm_gain.reshape(1, WIDTH), pick, pick_last)
    got = exchange(sent.reshape(EXPERTS, FULL, send_first), ALL).reshape(SLOTS, send_first)
    sent_rest = product(pick, normed_rest).astype(BF)
    got_rest = exchange(sent_rest.reshape(EXPERTS, FULL, rest), ALL).reshape(SLOTS, rest)
    gated, lifted, last = call(
        first_kernel, (SLOTS // TILE,),
        [
            tiled((TILE, send_first)), whole((WIDTH, hid)), whole((WIDTH, hid)), whole((hid, WIDTH)),
        ],
        [tiled((TILE, hid)), tiled((TILE, hid)), whole((SLOTS, PACK))],
        [shape((SLOTS, hid), F32), shape((SLOTS, hid), F32), shape((SLOTS, PACK), BF)], [nine],
        flops=4 * SLOTS * OUT_FIRST * hid, moved=SLOTS * (send_first + 4 * hid) * 2 + WIDTH * hid * 6,
    )(got, w_gate, w_up, w_down)
    activated, served = call(
        second_kernel, (SLOTS // TILE,),
        [
            tiled((TILE, rest)), whole((rest, hid), (OUT_FIRST // rest, 0)),
            whole((rest, hid), (OUT_FIRST // rest, 0)), whole((hid, BACK_FIRST)),
            tiled((TILE, hid)), tiled((TILE, hid)), tiled((TILE, PACK)),
        ],
        [tiled((TILE, hid)), tiled((TILE, back_first))],
        [shape((SLOTS, hid), BF), shape((SLOTS, back_first), BF)],
        flops=6 * SLOTS * rest * hid, moved=SLOTS * (rest + back_first + 4 * hid) * 2 + rest * hid * 6,
    )(got_rest, w_gate, w_up, w_down, gated, lifted, last)
    back = exchange(served.reshape(EXPERTS, FULL, back_first), ALL).reshape(SLOTS, back_first)
    served_rest = product(activated, w_down[:, BACK_FIRST:]).astype(BF)
    back_rest = exchange(
        served_rest.reshape(EXPERTS, FULL, WIDTH - BACK_FIRST), ALL
    ).reshape(SLOTS, WIDTH - BACK_FIRST)

    sums = product(split, back[:, :BACK_FIRST])
    nines = product(split_last, back[:, BACK_FIRST:].reshape(EXPERTS, WIDTH))
    base = residual + (nines[:tok] + nines[tok:])
    base = jnp.concatenate(
        [base[:, :BACK_FIRST] + (sums[:tok] + sums[tok:]), base[:, BACK_FIRST:]], axis=1
    )
    fixed = BACK_FIRST // FINISH
    out = call(
        finish_kernel, (WIDTH // FINISH,),
        [
            pl.BlockSpec((tok, FINISH), lambda i: (0, i)),
            whole((2 * tok, SLOTS)),
            pl.BlockSpec((SLOTS, FINISH), lambda i: (0, jnp.maximum(i - fixed, 0))),
        ],
        pl.BlockSpec((tok, FINISH), lambda i: (0, i)), shape((tok, WIDTH), BF),
        flops=4 * tok * SLOTS * WIDTH, moved=SLOTS * WIDTH * 2,
    )(base, split, back_rest)
    return out[None]


def solution(mesh):
    fine = Mesh(mesh.devices.reshape(4, 2, 2, 2, 4), ALL)
    return jax.shard_map(
        layer,
        mesh=fine,
        in_specs=(
            P(DP, CTX, None),
            P(DP, CTX, None),
            P(DP, CTX, None),
            P(DP, CTX, None),
            P(None, CTX),
            P(),
            P(DP, CTX, None),
            P(DP, CTX, None),
            P(ALL, None, None),
            P(ALL, None, None),
            P(ALL, None, None),
        ),
        out_specs=P(DP, CTX, None),
        check_vma=False,
    )
```

```python
import jax
import jax.numpy as jnp
from jax import lax
from jax.experimental import pallas as pl
from jax.experimental.pallas import tpu as pltpu
from jax.sharding import Mesh, PartitionSpec as P


KVH = 2
DH = 128
EXPERTS = 128
FULL = 8
SLOTS = EXPERTS * FULL
WIDTH = 4096
PACK = WIDTH // 8
FOUR = 4
HALF = WIDTH // 2
FIRST = HALF + PACK
TILE = 512

DP = ("z", "xl", "core")
CTX = ("xh", "y")
ALL = DP + CTX
BF = jnp.bfloat16
F32 = jnp.float32


def exchange(blocks, axes):
    return lax.all_to_all(blocks, axes, split_axis=0, concat_axis=0, tiled=True)


def neighbour_pairs():
    pairs = []
    for z in range(4):
        for xl in range(2):
            for core in range(2):
                for xh in range(2):
                    for y in range(4):
                        src = (((z * 2 + xl) * 2 + core) * 2 + xh) * 4 + y
                        dst = (((z * 2 + 1 - xl) * 2 + core) * 2 + 1 - xh) * 4 + y
                        pairs.append((src, dst))
    return pairs


def shift(block, step):
    return lax.ppermute(block, "y", [(i, (i + step) % 4) for i in range(4)])


def gather_pair(keys, values):
    pair = jnp.concatenate([keys, values], axis=1)
    gathered = exchange(jnp.broadcast_to(pair[None], (8,) + pair.shape), CTX)
    return gathered.reshape(8 * pair.shape[0], pair.shape[1])


def attend_kernel(place_ref, query_ref, key_ref, value_ref, out_ref, bias, flipped):
    tok = query_ref.shape[0]
    heads = query_ref.shape[1] // DH

    @pl.when(pl.program_id(0) == 0)
    def _():
        query_pos = place_ref[0] * tok + lax.broadcasted_iota(jnp.int32, bias.shape, 0)
        key_pos = lax.broadcasted_iota(jnp.int32, bias.shape, 1)
        bias[...] = jnp.where(key_pos <= query_pos, 0.0, -1e30)
        flipped[...] = key_ref[...].T

    for head in range(0, heads, 2):
        pair = [slice((head + i) * DH, (head + i + 1) * DH) for i in range(2)]
        rows = jnp.concatenate([query_ref[:, at] for at in pair], axis=0)
        scores = product(rows, flipped[...]) * DH ** (-0.5)
        scores = scores + jnp.concatenate([bias[...], bias[...]], axis=0)
        weights = jnp.exp(scores - jnp.max(scores, axis=1, keepdims=True))
        total = jnp.sum(weights, axis=1, keepdims=True)
        out = (product(weights.astype(BF), value_ref[...]) / total).astype(BF)
        for i, at in enumerate(pair):
            out_ref[:, at] = out[i * tok : (i + 1) * tok]


def attend(place, queries, gathered, head):
    tok = queries.shape[0]
    keys = gathered.shape[0]
    half = queries.shape[1] // KVH
    block = 4 * DH
    steps = half // block
    return pl.pallas_call(
        attend_kernel,
        grid_spec=pltpu.PrefetchScalarGridSpec(
            num_scalar_prefetch=1,
            grid=(steps,),
            in_specs=[
                pl.BlockSpec((tok, block), lambda i, p: (0, head * steps + i)),
                pl.BlockSpec((keys, DH), lambda i, p: (0, head)),
                pl.BlockSpec((keys, DH), lambda i, p: (0, KVH + head)),
            ],
            out_specs=pl.BlockSpec((tok, block), lambda i, p: (0, i)),
            scratch_shapes=[pltpu.VMEM((tok, keys), F32), pltpu.VMEM((DH, keys), BF)],
        ),
        out_shape=jax.ShapeDtypeStruct((tok, half), BF),
        compiler_params=pltpu.CompilerParams(vmem_limit_bytes=16 * 1024 * 1024),
        cost_estimate=pl.CostEstimate(
            flops=4 * tok * half * keys, bytes_accessed=4 * tok * half, transcendentals=tok * half * 8
        ),
    )(place, queries, gathered, gathered)


def own_kernel(*refs):
    *row_refs, weight_ref, out_ref = refs
    half = row_refs[0].shape[1]
    left = jnp.concatenate([ref[...] for ref in row_refs[0::2]], axis=0)
    right = jnp.concatenate([ref[...] for ref in row_refs[1::2]], axis=0)
    out = product(left, weight_ref[:half]) + product(right, weight_ref[half:])
    out_ref[...] = out.astype(BF)


def pair_kernel(core_ref, *refs):
    *row_refs, fetched_ref, other_ref, out_ref = refs
    left = jnp.concatenate([ref[...] for ref in row_refs[0::2]], axis=0)
    right = jnp.concatenate([ref[...] for ref in row_refs[1::2]], axis=0)
    swap = core_ref[0] == 1
    out = product(jnp.where(swap, right, left), fetched_ref[...])
    out = out + product(jnp.where(swap, left, right), other_ref[...])
    out_ref[...] = out.astype(BF)


def columns(rows, weight, core=None):
    flat = [part for pair in rows for part in pair]
    tok, half = flat[0].shape
    wide = weight[0].shape[1]
    count = len(rows) * tok
    body = own_kernel if core is None else pair_kernel
    scalars = [] if core is None else [core]
    block = 256
    return pl.pallas_call(
        body,
        grid=(wide // block,),
        in_specs=[pl.BlockSpec(memory_space=pltpu.SMEM)] * len(scalars)
        + [whole((tok, half))] * len(flat)
        + [pl.BlockSpec((w.shape[0], block), lambda i: (0, i)) for w in weight],
        out_specs=pl.BlockSpec((count, block), lambda i: (0, i)),
        out_shape=jax.ShapeDtypeStruct((count, wide), BF),
        compiler_params=pltpu.CompilerParams(vmem_limit_bytes=24 * 1024 * 1024),
        cost_estimate=pl.CostEstimate(
            flops=4 * count * half * wide, bytes_accessed=4 * half * wide + 4 * count * half, transcendentals=0
        ),
    )(*scalars, *flat, *weight)


def project(attended, out_weight):
    first, second = attended
    tok, half = first.shape
    core = lax.axis_index("core")
    mine = lax.dynamic_slice_in_dim(out_weight, core * half, half, axis=0)
    fetched = lax.ppermute(mine, ALL, neighbour_pairs())
    below_a, above_a = shift(first, 1), shift(first, -1)
    below_b, above_b = shift(second, 1), shift(second, -1)
    far_a = shift(below_a, 1)
    far_b = shift(above_b, -1)
    other = lax.ppermute(fetched, "core", [(0, 1), (1, 0)])
    near = [(first, second), (below_a, below_b), (above_a, above_b)]
    far = [(far_a, far_b)]
    which = core.reshape(1)
    near_own = columns(near, [out_weight])
    near_pair = columns(near, [fetched, other], which)
    near = jnp.concatenate([near_own, near_pair], axis=1)
    from_above = shift(near[tok : 2 * tok], -1)
    from_below = shift(near[2 * tok :], 1)
    far_own = columns(far, [out_weight])
    far_pair = columns(far, [fetched, other], which)
    from_far = shift(jnp.concatenate([far_own, far_pair], axis=1), 2)
    return [near[:tok], from_above, from_far, from_below]


def product(left, right):
    return jnp.dot(left, right, preferred_element_type=F32)


def shuffle(pieces, slots, packing):
    cut = lax.broadcasted_iota(jnp.int32, (128, 128), 0 if packing else 1)
    held = lax.broadcasted_iota(jnp.int32, (128, 128), 1 if packing else 0)
    expert, piece, slot = lax.div(cut, 8), lax.rem(lax.div(cut, slots), pieces), lax.rem(cut, slots)
    return ((piece * 16 + expert) * slots + slot == held).astype(F32).astype(BF)


def packed_rows(rows, pieces, slots):
    wide = WIDTH // pieces
    cut = jnp.concatenate([rows[:, wide * s : wide * (s + 1)] for s in range(pieces)], axis=0)
    return product(shuffle(pieces, slots, True), cut).astype(BF)


def whole_rows(packed, pieces, slots):
    cut = product(shuffle(pieces, slots, False), packed).astype(BF)
    return [cut[16 * slots * s : 16 * slots * (s + 1)] for s in range(pieces)]


def make_kernel(
    place_ref, here_ref, above_ref, far_ref, below_ref, hidden_ref, gain_ref, pick_ref, last_ref,
    out_ref, halves_ref, residual_ref, normed,
):
    step = pl.program_id(0)

    @pl.when(step == 0)
    def _():
        for ahead, ref in enumerate((here_ref, above_ref, far_ref, below_ref)):
            y = lax.rem(place_ref[2] + ahead, 4)
            for part in range(2):
                high = place_ref[1] if part == 0 else 1 - place_ref[1]
                at = pl.ds(pl.multiple_of((high * 4 + y) * PACK, PACK), PACK)
                projected = ref[:, part * PACK : (part + 1) * PACK].astype(F32)
                residual_ref[:, at] = hidden_ref[:, at].astype(F32) + projected
        residual = residual_ref[...]
        mean = jnp.mean(residual * residual, axis=1, keepdims=True)
        normed[...] = (residual * lax.rsqrt(mean + 1e-06) * gain_ref[...]).astype(BF)

        halves_ref[...] = jnp.concatenate([normed[:, :HALF], normed[:, HALF:]], axis=0)

    out_ref[:, :HALF] = product(pick_ref[...], halves_ref[...]).astype(BF)
    out_ref[:, HALF:] = packed_rows(product(last_ref[...], normed[...]).astype(BF), 8, 1)


def silu_product(gated, lifted):
    return (gated / (1.0 + jnp.exp(-gated)) * lifted).astype(BF)


def expert_kernel(got_ref, gate_ref, up_ref, down_ref, out_ref):
    groups = got_ref.shape[0] // 128
    with_last = got_ref.shape[1] > HALF
    low, high = [], []
    for g in range(groups):
        pieces = whole_rows(got_ref[128 * g : 128 * (g + 1), :HALF], 2, FOUR)
        low.append(pieces[0])
        high.append(pieces[1])
    if with_last:
        for g in range(groups):
            pieces = whole_rows(got_ref[128 * g : 128 * (g + 1), HALF:], 8, 1)
            low.append(jnp.concatenate(pieces[:4], axis=1))
            high.append(jnp.concatenate(pieces[4:], axis=1))
    low, high = jnp.concatenate(low, axis=0), jnp.concatenate(high, axis=0)
    gated = product(low, gate_ref[:HALF]) + product(high, gate_ref[HALF:])
    lifted = product(low, up_ref[:HALF]) + product(high, up_ref[HALF:])
    served = product(silu_product(gated, lifted), down_ref[...]).astype(BF)
    for g in range(groups):
        out_ref[128 * g : 128 * (g + 1), :HALF] = packed_rows(served[64 * g : 64 * (g + 1)], 2, FOUR)
    if with_last:
        for g in range(groups):
            at = 64 * groups + 16 * g
            out_ref[128 * g : 128 * (g + 1), HALF:] = packed_rows(served[at : at + 16], 8, 1)


def experts(got, w_gate, w_up, w_down):
    wide = got.shape[1]
    hid = w_gate.shape[1]
    rows = SLOTS * wide // WIDTH
    return pl.pallas_call(
        expert_kernel,
        grid=(SLOTS // TILE,),
        in_specs=[tiled((TILE, wide))]
        + [pl.BlockSpec(w.shape, lambda i: (0, 0), pipeline_mode=pl.Buffered(1)) for w in (w_gate, w_up, w_down)],
        out_specs=tiled((TILE, wide)),
        out_shape=jax.ShapeDtypeStruct((SLOTS, wide), BF),
        compiler_params=pltpu.CompilerParams(vmem_limit_bytes=60 * 1024 * 1024),
        cost_estimate=pl.CostEstimate(
            flops=6 * rows * WIDTH * hid, bytes_accessed=4 * SLOTS * wide + 6 * WIDTH * hid, transcendentals=rows * hid
        ),
    )(got, w_gate, w_up, w_down)


def finish_kernel(low_ref, high_ref, split_ref, back_ref, out_ref):
    step = pl.program_id(0)
    tok, wide = low_ref.shape
    sums = product(split_ref[...], back_ref[...])
    for piece, ref in enumerate((low_ref, high_ref)):
        part = sums[2 * tok * piece : 2 * tok * (piece + 1)]
        at = pl.ds(pl.multiple_of(piece * HALF + step * wide, wide), wide)
        out_ref[:, at] = (ref[...] + (part[:tok] + part[tok:])).astype(BF)


def whole(shape, index=(0, 0)):
    return pl.BlockSpec(shape, lambda i: index)


def tiled(shape):
    return pl.BlockSpec(shape, lambda i: (i, 0))


def two_terms(weigh):
    high = weigh.astype(BF)
    low = (weigh - high.astype(F32)).astype(BF)
    return jnp.concatenate([high, low], axis=0)


def slots_of(routes, slot_gates):
    tok = routes.shape[0]
    named = routes[:, :, None] == jnp.arange(EXPERTS, dtype=jnp.int32)[None, None, :]
    hit = jnp.any(named, axis=1)
    gate = jnp.sum(jnp.where(named, slot_gates[:, :, None], 0.0), axis=1)
    before = jnp.arange(tok)[None, :] < jnp.arange(tok)[:, None]
    rank = jnp.dot(before.astype(BF), hit.astype(BF), preferred_element_type=F32)
    return hit, jnp.where(hit, rank, -1.0), gate


def layer(
    hidden,
    queries,
    keys,
    values,
    out_weight,
    norm_gain,
    routes,
    slot_scores,
    gate_weight,
    up_weight,
    down_weight,
):
    tok, _ = hidden.shape[1:]
    place = jnp.stack([lax.axis_index(CTX), lax.axis_index("xh"), lax.axis_index("y")])
    gathered = gather_pair(keys[0], values[0])
    first = attend(place, queries[0], gathered, 0)
    second = attend(place, queries[0], gathered, 1)

    score_rows = slot_scores[0]
    slot_gates = score_rows / jnp.sum(score_rows, axis=1, keepdims=True)
    _, rank, gate = slots_of(routes[0], slot_gates)
    order = jnp.arange(8)
    piece, slot = order // FOUR, (order % FOUR).astype(F32)
    placed = rank.T[:, None, :]

    def picks(start):
        taken = placed == (slot + start)[None, :, None]
        parts = [taken & (piece == p)[None, :, None] for p in range(2)]
        return jnp.concatenate(parts, axis=2).astype(BF).reshape(SLOTS, 2 * tok)

    def weighs(start):
        taken = jnp.where(rank[:, :, None] == slot + start, gate[:, :, None], 0.0)
        parts = [jnp.where(piece == p, taken, 0.0).reshape(tok, SLOTS) for p in range(2)]
        return jnp.concatenate([two_terms(part) for part in parts], axis=0)

    pick, pick_rest, pick_last = picks(0.0), picks(4.0), (rank.T == float(FULL)).astype(BF)
    split, split_rest = weighs(0.0), weighs(4.0)
    split_last = two_terms(jnp.where(rank == float(FULL), gate, 0.0))

    columns_home = project((first, second), out_weight)

    shape = jax.ShapeDtypeStruct
    weights = gate_weight[0], up_weight[0], down_weight[0]

    def swap(rows):
        wide = rows.shape[1]
        return exchange(rows.reshape(EXPERTS, 8, wide), ALL).reshape(SLOTS, wide)

    sent, halves, residual = pl.pallas_call(
        make_kernel,
        name="make",
        grid_spec=pltpu.PrefetchScalarGridSpec(
            num_scalar_prefetch=1,
            grid=(SLOTS // 128,),
            in_specs=[pl.BlockSpec((tok, 2 * PACK), lambda i, p: (0, 0))] * 4
            + [
                pl.BlockSpec((tok, WIDTH), lambda i, p: (0, 0)),
                pl.BlockSpec((1, WIDTH), lambda i, p: (0, 0)),
                pl.BlockSpec((128, 2 * tok), lambda i, p: (i, 0)),
                pl.BlockSpec((16, tok), lambda i, p: (i, 0)),
            ],
            out_specs=[
                pl.BlockSpec((128, FIRST), lambda i, p: (i, 0)),
                pl.BlockSpec((2 * tok, HALF), lambda i, p: (0, 0)),
                pl.BlockSpec((tok, WIDTH), lambda i, p: (0, 0)),
            ],
            scratch_shapes=[pltpu.VMEM((tok, WIDTH), BF)],
        ),
        out_shape=[shape((SLOTS, FIRST), BF), shape((2 * tok, HALF), BF), shape((tok, WIDTH), F32)],
        compiler_params=pltpu.CompilerParams(vmem_limit_bytes=60 * 1024 * 1024),
        cost_estimate=pl.CostEstimate(
            flops=4 * SLOTS * tok * HALF, bytes_accessed=SLOTS * FIRST * 2, transcendentals=0
        ),
    )(place, *columns_home, hidden[0], norm_gain.reshape(1, WIDTH), pick, pick_last)
    got = swap(sent)
    got_rest = swap(product(pick_rest, halves).astype(BF))
    back = swap(experts(got, *weights))
    back_rest = swap(experts(got_rest, *weights))

    sums = product(split, back[:, :HALF])
    sums = sums.reshape(2, 2, tok, HALF)
    nines = product(split_last, back[:, HALF:].reshape(EXPERTS, WIDTH))
    base = residual + (nines[:tok] + nines[tok:])
    base = base + jnp.concatenate([sums[0, 0] + sums[0, 1], sums[1, 0] + sums[1, 1]], axis=1)
    steps = HALF // PACK
    out = pl.pallas_call(
        finish_kernel,
        name="finish",
        grid=(steps,),
        in_specs=[
            pl.BlockSpec((tok, PACK), lambda i: (0, i)),
            pl.BlockSpec((tok, PACK), lambda i: (0, i + steps)),
            whole((4 * tok, SLOTS)),
            pl.BlockSpec((SLOTS, PACK), lambda i: (0, i)),
        ],
        out_specs=whole((tok, WIDTH)),
        out_shape=shape((tok, WIDTH), BF),
        compiler_params=pltpu.CompilerParams(vmem_limit_bytes=24 * 1024 * 1024),
        cost_estimate=pl.CostEstimate(
            flops=8 * tok * SLOTS * HALF, bytes_accessed=SLOTS * HALF * 2 + tok * WIDTH * 6, transcendentals=0
        ),
    )(base, base, split_rest, back_rest)
    return out[None]


def solution(mesh):
    fine = Mesh(mesh.devices.reshape(4, 2, 2, 2, 4), ALL)
    return jax.shard_map(
        layer,
        mesh=fine,
        in_specs=(
            P(DP, CTX, None),
            P(DP, CTX, None),
            P(DP, CTX, None),
            P(DP, CTX, None),
            P(None, CTX),
            P(),
            P(DP, CTX, None),
            P(DP, CTX, None),
            P(ALL, None, None),
            P(ALL, None, None),
            P(ALL, None, None),
        ),
        out_specs=P(DP, CTX, None),
        check_vma=False,
    )
```

```python
import jax
import jax.numpy as jnp
from jax import lax
from jax.experimental import pallas as pl
from jax.experimental.pallas import tpu as pltpu
from jax.sharding import Mesh, PartitionSpec as P


KVH = 2
DH = 128
EXPERTS = 128
FULL = 8
SLOTS = EXPERTS * FULL
WIDTH = 4096
PACK = WIDTH // 8
FOUR = 4
HALF = WIDTH // 2
FIRST = HALF + PACK
TILE = 512

DP = ("z", "xl", "core")
CTX = ("xh", "y")
ALL = DP + CTX
BF = jnp.bfloat16
F32 = jnp.float32


def exchange(blocks, axes):
    return lax.all_to_all(blocks, axes, split_axis=0, concat_axis=0, tiled=True)


def neighbour_pairs():
    pairs = []
    for z in range(4):
        for xl in range(2):
            for core in range(2):
                for xh in range(2):
                    for y in range(4):
                        src = (((z * 2 + xl) * 2 + core) * 2 + xh) * 4 + y
                        dst = (((z * 2 + 1 - xl) * 2 + core) * 2 + 1 - xh) * 4 + y
                        pairs.append((src, dst))
    return pairs


def shift(block, step):
    return lax.ppermute(block, "y", [(i, (i + step) % 4) for i in range(4)])


def gather_pair(keys, values):
    pair = jnp.concatenate([keys, values], axis=1)
    blocks = [pair]
    for ahead in range(1, 8):
        pairs = []
        for index in range(8):
            xh, y = index // 4, index % 4
            pairs.append(((xh ^ (ahead // 4)) * 4 + (y + ahead) % 4, index))
        blocks.append(lax.ppermute(pair, CTX, pairs))
    return blocks


def attend_kernel(place_ref, query_ref, *refs):
    *block_refs, out_ref, bias, flipped, held = refs
    tok = query_ref.shape[0]
    heads = query_ref.shape[1] // DH

    @pl.when(pl.program_id(0) == 0)
    def _():
        query_pos = place_ref[0] * tok + lax.broadcasted_iota(jnp.int32, (tok, tok), 0)
        for ahead in range(8):
            high = place_ref[1] if ahead < 4 else 1 - place_ref[1]
            source = high * 4 + lax.rem(place_ref[2] + ahead, 4)
            key_pos = source * tok + lax.broadcasted_iota(jnp.int32, (tok, tok), 1)
            at = slice(ahead * tok, (ahead + 1) * tok)
            bias[:, at] = jnp.where(key_pos <= query_pos, 0.0, -1e30)
            flipped[:, at] = block_refs[2 * ahead][...].T
            held[at] = block_refs[2 * ahead + 1][...]

    for head in range(0, heads, 2):
        pair = [slice((head + i) * DH, (head + i + 1) * DH) for i in range(2)]
        rows = jnp.concatenate([query_ref[:, at] for at in pair], axis=0)
        scores = product(rows, flipped[...]) * DH ** (-0.5)
        scores = scores + jnp.concatenate([bias[...], bias[...]], axis=0)
        weights = jnp.exp(scores - jnp.max(scores, axis=1, keepdims=True))
        total = jnp.sum(weights, axis=1, keepdims=True)
        out = (product(weights.astype(BF), held[...]) / total).astype(BF)
        for i, at in enumerate(pair):
            out_ref[:, at] = out[i * tok : (i + 1) * tok]


def attend(place, queries, blocks, head):
    tok = queries.shape[0]
    keys = len(blocks) * tok
    half = queries.shape[1] // KVH
    block = 4 * DH
    steps = half // block
    specs = [
        pl.BlockSpec((tok, DH), lambda i, p: (0, head)),
        pl.BlockSpec((tok, DH), lambda i, p: (0, KVH + head)),
    ]
    return pl.pallas_call(
        attend_kernel,
        grid_spec=pltpu.PrefetchScalarGridSpec(
            num_scalar_prefetch=1,
            grid=(steps,),
            in_specs=[pl.BlockSpec((tok, block), lambda i, p: (0, head * steps + i))] + specs * len(blocks),
            out_specs=pl.BlockSpec((tok, block), lambda i, p: (0, i)),
            scratch_shapes=[
                pltpu.VMEM((tok, keys), F32), pltpu.VMEM((DH, keys), BF), pltpu.VMEM((keys, DH), BF)
            ],
        ),
        out_shape=jax.ShapeDtypeStruct((tok, half), BF),
        compiler_params=pltpu.CompilerParams(vmem_limit_bytes=16 * 1024 * 1024),
        cost_estimate=pl.CostEstimate(
            flops=4 * tok * half * keys, bytes_accessed=4 * tok * half, transcendentals=tok * half * 8
        ),
    )(place, queries, *[block for block in blocks for _ in range(2)])


def own_kernel(*refs):
    *row_refs, weight_ref, out_ref = refs
    half = row_refs[0].shape[1]
    left = jnp.concatenate([ref[...] for ref in row_refs[0::2]], axis=0)
    right = jnp.concatenate([ref[...] for ref in row_refs[1::2]], axis=0)
    out = product(left, weight_ref[:half]) + product(right, weight_ref[half:])
    out_ref[...] = out.astype(BF)


def pair_kernel(core_ref, *refs):
    *row_refs, fetched_ref, other_ref, out_ref = refs
    left = jnp.concatenate([ref[...] for ref in row_refs[0::2]], axis=0)
    right = jnp.concatenate([ref[...] for ref in row_refs[1::2]], axis=0)
    swap = core_ref[0] == 1
    out = product(jnp.where(swap, right, left), fetched_ref[...])
    out = out + product(jnp.where(swap, left, right), other_ref[...])
    out_ref[...] = out.astype(BF)


def columns(rows, weight, core=None):
    flat = [part for pair in rows for part in pair]
    tok, half = flat[0].shape
    wide = weight[0].shape[1]
    count = len(rows) * tok
    body = own_kernel if core is None else pair_kernel
    scalars = [] if core is None else [core]
    block = 256
    return pl.pallas_call(
        body,
        grid=(wide // block,),
        in_specs=[pl.BlockSpec(memory_space=pltpu.SMEM)] * len(scalars)
        + [whole((tok, half))] * len(flat)
        + [pl.BlockSpec((w.shape[0], block), lambda i: (0, i)) for w in weight],
        out_specs=pl.BlockSpec((count, block), lambda i: (0, i)),
        out_shape=jax.ShapeDtypeStruct((count, wide), BF),
        compiler_params=pltpu.CompilerParams(vmem_limit_bytes=24 * 1024 * 1024),
        cost_estimate=pl.CostEstimate(
            flops=4 * count * half * wide, bytes_accessed=4 * half * wide + 4 * count * half, transcendentals=0
        ),
    )(*scalars, *flat, *weight)


def project(attended, out_weight):
    first, second = attended
    tok, half = first.shape
    core = lax.axis_index("core")
    mine = lax.dynamic_slice_in_dim(out_weight, core * half, half, axis=0)
    fetched = lax.ppermute(mine, ALL, neighbour_pairs())
    below_a, above_a = shift(first, 1), shift(first, -1)
    below_b, above_b = shift(second, 1), shift(second, -1)
    far_a = shift(below_a, 1)
    far_b = shift(above_b, -1)
    other = lax.ppermute(fetched, "core", [(0, 1), (1, 0)])
    near = [(first, second), (below_a, below_b), (above_a, above_b)]
    far = [(far_a, far_b)]
    which = core.reshape(1)
    weight = out_weight
    near_own = columns(near, [weight])
    near_pair = columns(near, [fetched, other], which)
    near = jnp.concatenate([near_own, near_pair], axis=1)
    from_above = shift(near[tok : 2 * tok], -1)
    from_below = shift(near[2 * tok :], 1)
    far_own = columns(far, [weight])
    far_pair = columns(far, [fetched, other], which)
    from_far = shift(jnp.concatenate([far_own, far_pair], axis=1), 2)
    return [near[:tok], from_above, from_far, from_below]


def product(left, right):
    return jnp.dot(left, right, preferred_element_type=F32)


def shuffle(pieces, slots, packing):
    cut = lax.broadcasted_iota(jnp.int32, (128, 128), 0 if packing else 1)
    held = lax.broadcasted_iota(jnp.int32, (128, 128), 1 if packing else 0)
    expert, piece, slot = lax.div(cut, 8), lax.rem(lax.div(cut, slots), pieces), lax.rem(cut, slots)
    return ((piece * 16 + expert) * slots + slot == held).astype(F32).astype(BF)


def packed_rows(rows, pieces, slots):
    wide = WIDTH // pieces
    cut = jnp.concatenate([rows[:, wide * s : wide * (s + 1)] for s in range(pieces)], axis=0)
    return product(shuffle(pieces, slots, True), cut).astype(BF)


def whole_rows(packed, pieces, slots):
    cut = product(shuffle(pieces, slots, False), packed).astype(BF)
    return [cut[16 * slots * s : 16 * slots * (s + 1)] for s in range(pieces)]


def make_kernel(
    place_ref, here_ref, above_ref, far_ref, below_ref, hidden_ref, gain_ref, pick_ref, last_ref,
    out_ref, halves_ref, residual_ref, normed, last_rows,
):
    step = pl.program_id(0)

    @pl.when(step == 0)
    def _():
        for ahead, ref in enumerate((here_ref, above_ref, far_ref, below_ref)):
            y = lax.rem(place_ref[2] + ahead, 4)
            for part in range(2):
                high = place_ref[1] if part == 0 else 1 - place_ref[1]
                at = pl.ds(pl.multiple_of((high * 4 + y) * PACK, PACK), PACK)
                projected = ref[:, part * PACK : (part + 1) * PACK].astype(F32)
                residual_ref[:, at] = hidden_ref[:, at].astype(F32) + projected
        residual = residual_ref[...]
        mean = jnp.mean(residual * residual, axis=1, keepdims=True)
        normed[...] = (residual * lax.rsqrt(mean + 1e-06) * gain_ref[...]).astype(BF)

        halves_ref[...] = jnp.concatenate([normed[:, :HALF], normed[:, HALF:]], axis=0)
        last_rows[...] = product(last_ref[...], normed[...]).astype(BF)

    out_ref[:, :HALF] = product(pick_ref[...], halves_ref[...]).astype(BF)
    for i in range(2):
        rows = last_rows[pl.ds(pl.multiple_of(step * 32 + 16 * i, 16), 16), :]
        out_ref[128 * i : 128 * (i + 1), HALF:] = packed_rows(rows, 8, 1)


def silu_product(gated, lifted):
    return (gated / (1.0 + jnp.exp(-gated)) * lifted).astype(BF)


def expert_kernel(got_ref, gate_ref, up_ref, down_ref, out_ref):
    groups = got_ref.shape[0] // 128
    with_last = got_ref.shape[1] > HALF
    low, high = [], []
    for g in range(groups):
        pieces = whole_rows(got_ref[128 * g : 128 * (g + 1), :HALF], 2, FOUR)
        low.append(pieces[0])
        high.append(pieces[1])
    if with_last:
        for g in range(groups):
            pieces = whole_rows(got_ref[128 * g : 128 * (g + 1), HALF:], 8, 1)
            low.append(jnp.concatenate(pieces[:4], axis=1))
            high.append(jnp.concatenate(pieces[4:], axis=1))
    low, high = jnp.concatenate(low, axis=0), jnp.concatenate(high, axis=0)
    gated = product(low, gate_ref[:HALF]) + product(high, gate_ref[HALF:])
    lifted = product(low, up_ref[:HALF]) + product(high, up_ref[HALF:])
    served = product(silu_product(gated, lifted), down_ref[...]).astype(BF)
    for g in range(groups):
        out_ref[128 * g : 128 * (g + 1), :HALF] = packed_rows(served[64 * g : 64 * (g + 1)], 2, FOUR)
    if with_last:
        for g in range(groups):
            at = 64 * groups + 16 * g
            out_ref[128 * g : 128 * (g + 1), HALF:] = packed_rows(served[at : at + 16], 8, 1)


def experts(got, w_gate, w_up, w_down):
    wide = got.shape[1]
    hid = w_gate.shape[1]
    rows = SLOTS * wide // WIDTH
    return pl.pallas_call(
        expert_kernel,
        grid=(SLOTS // TILE,),
        in_specs=[tiled((TILE, wide))]
        + [pl.BlockSpec(w.shape, lambda i: (0, 0), pipeline_mode=pl.Buffered(1)) for w in (w_gate, w_up, w_down)],
        out_specs=tiled((TILE, wide)),
        out_shape=jax.ShapeDtypeStruct((SLOTS, wide), BF),
        compiler_params=pltpu.CompilerParams(vmem_limit_bytes=60 * 1024 * 1024),
        cost_estimate=pl.CostEstimate(
            flops=6 * rows * WIDTH * hid, bytes_accessed=4 * SLOTS * wide + 6 * WIDTH * hid, transcendentals=rows * hid
        ),
    )(got, w_gate, w_up, w_down)


def finish_kernel(low_ref, high_ref, split_ref, back_ref, out_ref):
    step = pl.program_id(0)
    tok, wide = low_ref.shape
    sums = product(split_ref[...], back_ref[...])
    for piece, ref in enumerate((low_ref, high_ref)):
        part = sums[2 * tok * piece : 2 * tok * (piece + 1)]
        at = pl.ds(pl.multiple_of(piece * HALF + step * wide, wide), wide)
        out_ref[:, at] = (ref[...] + (part[:tok] + part[tok:])).astype(BF)


def whole(shape, index=(0, 0)):
    return pl.BlockSpec(shape, lambda i: index)


def tiled(shape):
    return pl.BlockSpec(shape, lambda i: (i, 0))


def two_terms(weigh):
    high = weigh.astype(BF)
    low = (weigh - high.astype(F32)).astype(BF)
    return jnp.concatenate([high, low], axis=0)


def slots_of(routes, slot_gates):
    tok = routes.shape[0]
    named = routes[:, :, None] == jnp.arange(EXPERTS, dtype=jnp.int32)[None, None, :]
    hit = jnp.any(named, axis=1)
    gate = jnp.sum(jnp.where(named, slot_gates[:, :, None], 0.0), axis=1)
    before = jnp.arange(tok)[None, :] < jnp.arange(tok)[:, None]
    rank = jnp.dot(before.astype(BF), hit.astype(BF), preferred_element_type=F32)
    return hit, jnp.where(hit, rank, -1.0), gate


def layer(
    hidden,
    queries,
    keys,
    values,
    out_weight,
    norm_gain,
    routes,
    slot_scores,
    gate_weight,
    up_weight,
    down_weight,
):
    tok, _ = hidden.shape[1:]
    place = jnp.stack([lax.axis_index(CTX), lax.axis_index("xh"), lax.axis_index("y")])
    gathered = gather_pair(keys[0], values[0])
    first = attend(place, queries[0], gathered, 0)
    second = attend(place, queries[0], gathered, 1)

    score_rows = slot_scores[0]
    slot_gates = score_rows / jnp.sum(score_rows, axis=1, keepdims=True)
    _, rank, gate = slots_of(routes[0], slot_gates)
    order = jnp.arange(8)
    piece, slot = order // FOUR, (order % FOUR).astype(F32)
    placed = rank.T[:, None, :]

    def picks(start):
        taken = placed == (slot + start)[None, :, None]
        parts = [taken & (piece == p)[None, :, None] for p in range(2)]
        return jnp.concatenate(parts, axis=2).astype(BF).reshape(SLOTS, 2 * tok)

    def weighs(start):
        taken = jnp.where(rank[:, :, None] == slot + start, gate[:, :, None], 0.0)
        parts = [jnp.where(piece == p, taken, 0.0).reshape(tok, SLOTS) for p in range(2)]
        return jnp.concatenate([two_terms(part) for part in parts], axis=0)

    pick, pick_rest, pick_last = picks(0.0), picks(4.0), (rank.T == float(FULL)).astype(BF)
    split, split_rest = weighs(0.0), weighs(4.0)
    split_last = two_terms(jnp.where(rank == float(FULL), gate, 0.0))

    columns_home = project((first, second), out_weight)

    shape = jax.ShapeDtypeStruct
    weights = gate_weight[0], up_weight[0], down_weight[0]

    def swap(rows):
        wide = rows.shape[1]
        return exchange(rows.reshape(EXPERTS, 8, wide), ALL).reshape(SLOTS, wide)

    sent, halves, residual = pl.pallas_call(
        make_kernel,
        name="make",
        grid_spec=pltpu.PrefetchScalarGridSpec(
            num_scalar_prefetch=1,
            grid=(SLOTS // 256,),
            in_specs=[pl.BlockSpec((tok, 2 * PACK), lambda i, p: (0, 0))] * 4
            + [
                pl.BlockSpec((tok, WIDTH), lambda i, p: (0, 0)),
                pl.BlockSpec((1, WIDTH), lambda i, p: (0, 0)),
                pl.BlockSpec((256, 2 * tok), lambda i, p: (i, 0)),
                pl.BlockSpec((EXPERTS, tok), lambda i, p: (0, 0)),
            ],
            out_specs=[
                pl.BlockSpec((256, FIRST), lambda i, p: (i, 0)),
                pl.BlockSpec((2 * tok, HALF), lambda i, p: (0, 0)),
                pl.BlockSpec((tok, WIDTH), lambda i, p: (0, 0)),
            ],
            scratch_shapes=[pltpu.VMEM((tok, WIDTH), BF), pltpu.VMEM((EXPERTS, WIDTH), BF)],
        ),
        out_shape=[shape((SLOTS, FIRST), BF), shape((2 * tok, HALF), BF), shape((tok, WIDTH), F32)],
        compiler_params=pltpu.CompilerParams(vmem_limit_bytes=57 * 1024 * 1024),
        cost_estimate=pl.CostEstimate(
            flops=4 * SLOTS * tok * HALF, bytes_accessed=SLOTS * FIRST * 2, transcendentals=0
        ),
    )(place, *columns_home, hidden[0], norm_gain.reshape(1, WIDTH), pick, pick_last)
    got = swap(sent)
    got_rest = swap(product(pick_rest, halves).astype(BF))
    back = swap(experts(got, *weights))
    back_rest = swap(experts(got_rest, *weights))

    sums = product(split, back[:, :HALF])
    sums = sums.reshape(2, 2, tok, HALF)
    nines = product(split_last, back[:, HALF:].reshape(EXPERTS, WIDTH))
    base = residual + (nines[:tok] + nines[tok:])
    base = base + jnp.concatenate([sums[0, 0] + sums[0, 1], sums[1, 0] + sums[1, 1]], axis=1)
    steps = HALF // PACK
    out = pl.pallas_call(
        finish_kernel,
        name="finish",
        grid=(steps,),
        in_specs=[
            pl.BlockSpec((tok, PACK), lambda i: (0, i)),
            pl.BlockSpec((tok, PACK), lambda i: (0, i + steps)),
            whole((4 * tok, SLOTS)),
            pl.BlockSpec((SLOTS, PACK), lambda i: (0, i)),
        ],
        out_specs=whole((tok, WIDTH)),
        out_shape=shape((tok, WIDTH), BF),
        compiler_params=pltpu.CompilerParams(vmem_limit_bytes=24 * 1024 * 1024),
        cost_estimate=pl.CostEstimate(
            flops=8 * tok * SLOTS * HALF, bytes_accessed=SLOTS * HALF * 2 + tok * WIDTH * 6, transcendentals=0
        ),
    )(base, base, split_rest, back_rest)
    return out[None]


def solution(mesh):
    fine = Mesh(mesh.devices.reshape(4, 2, 2, 2, 4), ALL)
    return jax.shard_map(
        layer,
        mesh=fine,
        in_specs=(
            P(DP, CTX, None),
            P(DP, CTX, None),
            P(DP, CTX, None),
            P(DP, CTX, None),
            P(None, CTX),
            P(),
            P(DP, CTX, None),
            P(DP, CTX, None),
            P(ALL, None, None),
            P(ALL, None, None),
            P(ALL, None, None),
        ),
        out_specs=P(DP, CTX, None),
        check_vma=False,
    )
```

```python
import jax
import jax.numpy as jnp
from jax import lax
from jax.experimental import pallas as pl
from jax.experimental.pallas import tpu as pltpu
from jax.sharding import Mesh, PartitionSpec as P


KVH = 2
DH = 128
TOP = 8
EXPERTS = 128
FULL = 8
SLOTS = EXPERTS * FULL
WIDTH = 4096
PACK = WIDTH // 8
FOUR = 4
HALF = WIDTH // 2
FIRST = HALF + PACK
TILE = 512

DP = ("z", "xl", "core")
CTX = ("xh", "y")
ALL = DP + CTX
BF = jnp.bfloat16
F32 = jnp.float32


def exchange(blocks, axes):
    return lax.all_to_all(blocks, axes, split_axis=0, concat_axis=0, tiled=True)


def neighbour_pairs():
    pairs = []
    for z in range(4):
        for xl in range(2):
            for core in range(2):
                for xh in range(2):
                    for y in range(4):
                        src = (((z * 2 + xl) * 2 + core) * 2 + xh) * 4 + y
                        dst = (((z * 2 + 1 - xl) * 2 + core) * 2 + 1 - xh) * 4 + y
                        pairs.append((src, dst))
    return pairs


def shift(block, step):
    return lax.ppermute(block, "y", [(i, (i + step) % 4) for i in range(4)])


def gather_pair(keys, values):
    pair = jnp.concatenate([keys, values], axis=1)
    blocks = [pair]
    for ahead in range(1, 8):
        pairs = []
        for index in range(8):
            xh, y = index // 4, index % 4
            pairs.append(((xh ^ (ahead // 4)) * 4 + (y + ahead) % 4, index))
        blocks.append(lax.ppermute(pair, CTX, pairs))
    return blocks


def attend_kernel(place_ref, query_ref, *refs):
    *block_refs, out_ref, bias, flipped, held = refs
    tok = query_ref.shape[0]
    heads = query_ref.shape[1] // DH

    @pl.when(pl.program_id(0) == 0)
    def _():
        query_pos = place_ref[0] * tok + lax.broadcasted_iota(jnp.int32, (tok, tok), 0)
        for ahead in range(8):
            high = place_ref[1] if ahead < 4 else 1 - place_ref[1]
            source = high * 4 + lax.rem(place_ref[2] + ahead, 4)
            key_pos = source * tok + lax.broadcasted_iota(jnp.int32, (tok, tok), 1)
            at = slice(ahead * tok, (ahead + 1) * tok)
            bias[:, at] = jnp.where(key_pos <= query_pos, 0.0, -1e30)
            flipped[:, at] = block_refs[2 * ahead][...].T
            held[at] = block_refs[2 * ahead + 1][...]

    for head in range(0, heads, 2):
        pair = [slice((head + i) * DH, (head + i + 1) * DH) for i in range(2)]
        rows = jnp.concatenate([query_ref[:, at] for at in pair], axis=0)
        scores = product(rows, flipped[...]) * DH ** (-0.5)
        scores = scores + jnp.concatenate([bias[...], bias[...]], axis=0)
        weights = jnp.exp(scores - jnp.max(scores, axis=1, keepdims=True))
        total = jnp.sum(weights, axis=1, keepdims=True)
        out = (product(weights.astype(BF), held[...]) / total).astype(BF)
        for i, at in enumerate(pair):
            out_ref[:, at] = out[i * tok : (i + 1) * tok]


def attend(place, queries, blocks, head):
    tok = queries.shape[0]
    keys = len(blocks) * tok
    half = queries.shape[1] // KVH
    block = 4 * DH
    steps = half // block
    specs = [
        pl.BlockSpec((tok, DH), lambda i, p: (0, head)),
        pl.BlockSpec((tok, DH), lambda i, p: (0, KVH + head)),
    ]
    return pl.pallas_call(
        attend_kernel,
        grid_spec=pltpu.PrefetchScalarGridSpec(
            num_scalar_prefetch=1,
            grid=(steps,),
            in_specs=[pl.BlockSpec((tok, block), lambda i, p: (0, head * steps + i))] + specs * len(blocks),
            out_specs=pl.BlockSpec((tok, block), lambda i, p: (0, i)),
            scratch_shapes=[
                pltpu.VMEM((tok, keys), F32), pltpu.VMEM((DH, keys), BF), pltpu.VMEM((keys, DH), BF)
            ],
        ),
        out_shape=jax.ShapeDtypeStruct((tok, half), BF),
        compiler_params=pltpu.CompilerParams(vmem_limit_bytes=16 * 1024 * 1024),
        cost_estimate=pl.CostEstimate(
            flops=4 * tok * half * keys, bytes_accessed=4 * tok * half, transcendentals=tok * half * 8
        ),
    )(place, queries, *[block for block in blocks for _ in range(2)])


def own_kernel(*refs):
    *row_refs, weight_ref, out_ref = refs
    half = row_refs[0].shape[1]
    left = jnp.concatenate([ref[...] for ref in row_refs[0::2]], axis=0)
    right = jnp.concatenate([ref[...] for ref in row_refs[1::2]], axis=0)
    out = product(left, weight_ref[:half]) + product(right, weight_ref[half:])
    out_ref[...] = out.astype(BF)


def pair_kernel(core_ref, *refs):
    *row_refs, fetched_ref, other_ref, out_ref = refs
    left = jnp.concatenate([ref[...] for ref in row_refs[0::2]], axis=0)
    right = jnp.concatenate([ref[...] for ref in row_refs[1::2]], axis=0)
    swap = core_ref[0] == 1
    out = product(jnp.where(swap, right, left), fetched_ref[...])
    out = out + product(jnp.where(swap, left, right), other_ref[...])
    out_ref[...] = out.astype(BF)


def columns(rows, weight, core=None):
    flat = [part for pair in rows for part in pair]
    tok, half = flat[0].shape
    wide = weight[0].shape[1]
    count = len(rows) * tok
    body = own_kernel if core is None else pair_kernel
    scalars = [] if core is None else [core]
    block = 256
    return pl.pallas_call(
        body,
        grid=(wide // block,),
        in_specs=[pl.BlockSpec(memory_space=pltpu.SMEM)] * len(scalars)
        + [whole((tok, half))] * len(flat)
        + [pl.BlockSpec((w.shape[0], block), lambda i: (0, i)) for w in weight],
        out_specs=pl.BlockSpec((count, block), lambda i: (0, i)),
        out_shape=jax.ShapeDtypeStruct((count, wide), BF),
        compiler_params=pltpu.CompilerParams(vmem_limit_bytes=24 * 1024 * 1024),
        cost_estimate=pl.CostEstimate(
            flops=4 * count * half * wide, bytes_accessed=4 * half * wide + 4 * count * half, transcendentals=0
        ),
    )(*scalars, *flat, *weight)


def project(attended, out_weight):
    first, second = attended
    tok, half = first.shape
    core = lax.axis_index("core")
    mine = lax.dynamic_slice_in_dim(out_weight, core * half, half, axis=0)
    fetched = lax.ppermute(mine, ALL, neighbour_pairs())
    below_a, above_a = shift(first, 1), shift(first, -1)
    below_b, above_b = shift(second, 1), shift(second, -1)
    far_a = shift(below_a, 1)
    far_b = shift(above_b, -1)
    other = lax.ppermute(fetched, "core", [(0, 1), (1, 0)])
    near = [(first, second), (below_a, below_b), (above_a, above_b)]
    far = [(far_a, far_b)]
    which = core.reshape(1)
    weight = out_weight
    near_own = columns(near, [weight])
    near_pair = columns(near, [fetched, other], which)
    near = jnp.concatenate([near_own, near_pair], axis=1)
    from_above = shift(near[tok : 2 * tok], -1)
    from_below = shift(near[2 * tok :], 1)
    far_own = columns(far, [weight])
    far_pair = columns(far, [fetched, other], which)
    from_far = shift(jnp.concatenate([far_own, far_pair], axis=1), 2)
    return [near[:tok], from_above, from_far, from_below]


def product(left, right):
    return jnp.dot(left, right, preferred_element_type=F32)


def shuffle(pieces, slots, packing):
    cut = lax.broadcasted_iota(jnp.int32, (128, 128), 0 if packing else 1)
    held = lax.broadcasted_iota(jnp.int32, (128, 128), 1 if packing else 0)
    expert, piece, slot = lax.div(cut, 8), lax.rem(lax.div(cut, slots), pieces), lax.rem(cut, slots)
    return ((piece * 16 + expert) * slots + slot == held).astype(F32).astype(BF)


def packed_rows(rows, pieces, slots):
    wide = WIDTH // pieces
    cut = jnp.concatenate([rows[:, wide * s : wide * (s + 1)] for s in range(pieces)], axis=0)
    return product(shuffle(pieces, slots, True), cut).astype(BF)


def whole_rows(packed, pieces, slots):
    cut = product(shuffle(pieces, slots, False), packed).astype(BF)
    return [cut[16 * slots * s : 16 * slots * (s + 1)] for s in range(pieces)]


def make_kernel(
    place_ref, here_ref, above_ref, far_ref, below_ref, hidden_ref, gain_ref, pick_ref, last_ref,
    out_ref, halves_ref, residual_ref, normed, last_rows,
):
    step = pl.program_id(0)

    @pl.when(step == 0)
    def _():
        for ahead, ref in enumerate((here_ref, above_ref, far_ref, below_ref)):
            y = lax.rem(place_ref[2] + ahead, 4)
            for part in range(2):
                high = place_ref[1] if part == 0 else 1 - place_ref[1]
                at = pl.ds(pl.multiple_of((high * 4 + y) * PACK, PACK), PACK)
                projected = ref[:, part * PACK : (part + 1) * PACK].astype(F32)
                residual_ref[:, at] = hidden_ref[:, at].astype(F32) + projected
        residual = residual_ref[...]
        mean = jnp.mean(residual * residual, axis=1, keepdims=True)
        normed[...] = (residual * lax.rsqrt(mean + 1e-06) * gain_ref[...]).astype(BF)

        halves_ref[...] = jnp.concatenate([normed[:, :HALF], normed[:, HALF:]], axis=0)
        last_rows[...] = product(last_ref[...], normed[...]).astype(BF)

    out_ref[:, :HALF] = product(pick_ref[...], halves_ref[...]).astype(BF)
    for i in range(2):
        rows = last_rows[pl.ds(pl.multiple_of(step * 32 + 16 * i, 16), 16), :]
        out_ref[128 * i : 128 * (i + 1), HALF:] = packed_rows(rows, 8, 1)


def silu_product(gated, lifted):
    return (gated / (1.0 + jnp.exp(-gated)) * lifted).astype(BF)


def expert_kernel(got_ref, gate_ref, up_ref, down_ref, out_ref):
    groups = got_ref.shape[0] // 128
    with_last = got_ref.shape[1] > HALF
    low, high = [], []
    for g in range(groups):
        pieces = whole_rows(got_ref[128 * g : 128 * (g + 1), :HALF], 2, FOUR)
        low.append(pieces[0])
        high.append(pieces[1])
    if with_last:
        for g in range(groups):
            pieces = whole_rows(got_ref[128 * g : 128 * (g + 1), HALF:], 8, 1)
            low.append(jnp.concatenate(pieces[:4], axis=1))
            high.append(jnp.concatenate(pieces[4:], axis=1))
    low, high = jnp.concatenate(low, axis=0), jnp.concatenate(high, axis=0)
    gated = product(low, gate_ref[:HALF]) + product(high, gate_ref[HALF:])
    lifted = product(low, up_ref[:HALF]) + product(high, up_ref[HALF:])
    served = product(silu_product(gated, lifted), down_ref[...]).astype(BF)
    for g in range(groups):
        out_ref[128 * g : 128 * (g + 1), :HALF] = packed_rows(served[64 * g : 64 * (g + 1)], 2, FOUR)
    if with_last:
        for g in range(groups):
            at = 64 * groups + 16 * g
            out_ref[128 * g : 128 * (g + 1), HALF:] = packed_rows(served[at : at + 16], 8, 1)


def experts(got, w_gate, w_up, w_down):
    wide = got.shape[1]
    hid = w_gate.shape[1]
    rows = SLOTS * wide // WIDTH
    return pl.pallas_call(
        expert_kernel,
        grid=(SLOTS // TILE,),
        in_specs=[tiled((TILE, wide))]
        + [pl.BlockSpec(w.shape, lambda i: (0, 0), pipeline_mode=pl.Buffered(1)) for w in (w_gate, w_up, w_down)],
        out_specs=tiled((TILE, wide)),
        out_shape=jax.ShapeDtypeStruct((SLOTS, wide), BF),
        compiler_params=pltpu.CompilerParams(vmem_limit_bytes=60 * 1024 * 1024),
        cost_estimate=pl.CostEstimate(
            flops=6 * rows * WIDTH * hid, bytes_accessed=4 * SLOTS * wide + 6 * WIDTH * hid, transcendentals=rows * hid
        ),
    )(got, w_gate, w_up, w_down)


def finish_kernel(low_ref, high_ref, split_ref, back_ref, out_ref):
    step = pl.program_id(0)
    tok, wide = low_ref.shape
    sums = product(split_ref[...], back_ref[...])
    for piece, ref in enumerate((low_ref, high_ref)):
        part = sums[2 * tok * piece : 2 * tok * (piece + 1)]
        at = pl.ds(pl.multiple_of(piece * HALF + step * wide, wide), wide)
        out_ref[:, at] = (ref[...] + (part[:tok] + part[tok:])).astype(BF)


def whole(shape, index=(0, 0)):
    return pl.BlockSpec(shape, lambda i: index)


def tiled(shape):
    return pl.BlockSpec(shape, lambda i: (i, 0))


def prep_kernel(routes_ref, scores_ref, pick_ref, pick_rest_ref, pick_last_ref, split_ref, split_rest_ref, split_last_ref):
    tok = routes_ref.shape[0]
    scores = scores_ref[...]
    gates = scores / jnp.sum(scores, axis=1, keepdims=True)
    expert = lax.broadcasted_iota(jnp.int32, (tok, EXPERTS), 1)
    hit = jnp.zeros((tok, EXPERTS), F32)
    gate = jnp.zeros((tok, EXPERTS), F32)
    for k in range(TOP):
        named = routes_ref[:, k : k + 1] == expert
        hit = hit + jnp.where(named, 1.0, 0.0)
        gate = gate + jnp.where(named, gates[:, k : k + 1], 0.0)
    row = lax.broadcasted_iota(jnp.int32, (tok, tok), 0)
    col = lax.broadcasted_iota(jnp.int32, (tok, tok), 1)
    earlier = product(jnp.where(col < row, 1.0, 0.0).astype(BF), hit.astype(BF))
    rank = jnp.where(hit > 0.0, earlier, -1.0)

    placed = jnp.broadcast_to(rank.T[:, None, :], (EXPERTS, 8, tok))
    order = lax.broadcasted_iota(jnp.int32, (EXPERTS, 8, tok), 1)
    for start, ref in ((0, pick_ref), (FOUR, pick_rest_ref)):
        taken = placed == (lax.rem(order, FOUR) + start).astype(F32)
        for p in range(2):
            part = jnp.where(taken & (lax.div(order, FOUR) == p), 1.0, 0.0)
            ref[:, p * tok : (p + 1) * tok] = part.reshape(SLOTS, tok).astype(BF)
    pick_last_ref[...] = jnp.where(rank.T == float(FULL), 1.0, 0.0).astype(BF)

    lane = lax.broadcasted_iota(jnp.int32, (EXPERTS, SLOTS), 1)
    own = lax.broadcasted_iota(jnp.int32, (EXPERTS, SLOTS), 0)
    spread = jnp.where(lax.div(lane, 8) == own, 1.0, 0.0).astype(BF)
    high = gate.astype(BF)
    terms = jnp.concatenate([high, (gate - high.astype(F32)).astype(BF)], axis=0)
    weigh = product(terms, spread)
    ranks = product(rank.astype(BF), spread)
    ranks = jnp.concatenate([ranks, ranks], axis=0)
    order = lax.rem(lax.broadcasted_iota(jnp.int32, (2 * tok, SLOTS), 1), 8)
    for start, ref in ((0, split_ref), (FOUR, split_rest_ref)):
        taken = ranks == (lax.rem(order, FOUR) + start).astype(F32)
        for p in range(2):
            part = jnp.where(taken & (lax.div(order, FOUR) == p), weigh, 0.0)
            ref[2 * tok * p : 2 * tok * (p + 1)] = part.astype(BF)
    last = jnp.concatenate([rank, rank], axis=0) == float(FULL)
    split_last_ref[...] = jnp.where(last, terms.astype(F32), 0.0).astype(BF)


def prep(routes, scores):
    tok = routes.shape[0]
    shapes = [(SLOTS, 2 * tok), (SLOTS, 2 * tok), (EXPERTS, tok), (4 * tok, SLOTS), (4 * tok, SLOTS), (2 * tok, EXPERTS)]
    vmem = pl.BlockSpec(memory_space=pltpu.VMEM)
    return pl.pallas_call(
        prep_kernel,
        name="prep",
        in_specs=[vmem] * 2,
        out_specs=[vmem] * len(shapes),
        out_shape=[jax.ShapeDtypeStruct(shape, BF) for shape in shapes],
        compiler_params=pltpu.CompilerParams(vmem_limit_bytes=24 * 1024 * 1024),
        cost_estimate=pl.CostEstimate(flops=2 * 10**8, bytes_accessed=3 * 10**6, transcendentals=0),
    )(routes, scores)


def layer(
    hidden,
    queries,
    keys,
    values,
    out_weight,
    norm_gain,
    routes,
    slot_scores,
    gate_weight,
    up_weight,
    down_weight,
):
    tok, _ = hidden.shape[1:]
    place = jnp.stack([lax.axis_index(CTX), lax.axis_index("xh"), lax.axis_index("y")])
    gathered = gather_pair(keys[0], values[0])
    first = attend(place, queries[0], gathered, 0)
    second = attend(place, queries[0], gathered, 1)

    pick, pick_rest, pick_last, split, split_rest, split_last = prep(routes[0], slot_scores[0])

    columns_home = project((first, second), out_weight)

    shape = jax.ShapeDtypeStruct
    weights = gate_weight[0], up_weight[0], down_weight[0]

    def swap(rows):
        wide = rows.shape[1]
        return exchange(rows.reshape(EXPERTS, 8, wide), ALL).reshape(SLOTS, wide)

    sent, halves, residual = pl.pallas_call(
        make_kernel,
        name="make",
        grid_spec=pltpu.PrefetchScalarGridSpec(
            num_scalar_prefetch=1,
            grid=(SLOTS // 256,),
            in_specs=[pl.BlockSpec((tok, 2 * PACK), lambda i, p: (0, 0))] * 4
            + [
                pl.BlockSpec((tok, WIDTH), lambda i, p: (0, 0)),
                pl.BlockSpec((1, WIDTH), lambda i, p: (0, 0)),
                pl.BlockSpec((256, 2 * tok), lambda i, p: (i, 0)),
                pl.BlockSpec((EXPERTS, tok), lambda i, p: (0, 0)),
            ],
            out_specs=[
                pl.BlockSpec((256, FIRST), lambda i, p: (i, 0)),
                pl.BlockSpec((2 * tok, HALF), lambda i, p: (0, 0)),
                pl.BlockSpec((tok, WIDTH), lambda i, p: (0, 0)),
            ],
            scratch_shapes=[pltpu.VMEM((tok, WIDTH), BF), pltpu.VMEM((EXPERTS, WIDTH), BF)],
        ),
        out_shape=[shape((SLOTS, FIRST), BF), shape((2 * tok, HALF), BF), shape((tok, WIDTH), F32)],
        compiler_params=pltpu.CompilerParams(vmem_limit_bytes=57 * 1024 * 1024),
        cost_estimate=pl.CostEstimate(
            flops=4 * SLOTS * tok * HALF, bytes_accessed=SLOTS * FIRST * 2, transcendentals=0
        ),
    )(place, *columns_home, hidden[0], norm_gain.reshape(1, WIDTH), pick, pick_last)
    got = swap(sent)
    got_rest = swap(product(pick_rest, halves).astype(BF))
    back = swap(experts(got, *weights))
    back_rest = swap(experts(got_rest, *weights))

    sums = product(split, back[:, :HALF])
    sums = sums.reshape(2, 2, tok, HALF)
    nines = product(split_last, back[:, HALF:].reshape(EXPERTS, WIDTH))
    base = residual + (nines[:tok] + nines[tok:])
    base = base + jnp.concatenate([sums[0, 0] + sums[0, 1], sums[1, 0] + sums[1, 1]], axis=1)
    steps = HALF // PACK
    out = pl.pallas_call(
        finish_kernel,
        name="finish",
        grid=(steps,),
        in_specs=[
            pl.BlockSpec((tok, PACK), lambda i: (0, i)),
            pl.BlockSpec((tok, PACK), lambda i: (0, i + steps)),
            whole((4 * tok, SLOTS)),
            pl.BlockSpec((SLOTS, PACK), lambda i: (0, i)),
        ],
        out_specs=whole((tok, WIDTH)),
        out_shape=shape((tok, WIDTH), BF),
        compiler_params=pltpu.CompilerParams(vmem_limit_bytes=24 * 1024 * 1024),
        cost_estimate=pl.CostEstimate(
            flops=8 * tok * SLOTS * HALF, bytes_accessed=SLOTS * HALF * 2 + tok * WIDTH * 6, transcendentals=0
        ),
    )(base, base, split_rest, back_rest)
    return out[None]


def solution(mesh):
    fine = Mesh(mesh.devices.reshape(4, 2, 2, 2, 4), ALL)
    return jax.shard_map(
        layer,
        mesh=fine,
        in_specs=(
            P(DP, CTX, None),
            P(DP, CTX, None),
            P(DP, CTX, None),
            P(DP, CTX, None),
            P(None, CTX),
            P(),
            P(DP, CTX, None),
            P(DP, CTX, None),
            P(ALL, None, None),
            P(ALL, None, None),
            P(ALL, None, None),
        ),
        out_specs=P(DP, CTX, None),
        check_vma=False,
    )
```

```python
import functools

import jax
import jax.numpy as jnp
from jax import lax
from jax.experimental import pallas as pl
from jax.experimental.pallas import tpu as pltpu
from jax.sharding import Mesh, PartitionSpec as P


KVH = 2
DH = 128
TOP = 8
EXPERTS = 128
FULL = 8
SLOTS = EXPERTS * FULL
WIDTH = 4096
PACK = WIDTH // 8
FOUR = 4
HALF = WIDTH // 2
FIRST = HALF + PACK
TILE = 512
COLUMNS = 256

DP = ("z", "xl", "core")
CTX = ("xh", "y")
ALL = DP + CTX
BF = jnp.bfloat16
F32 = jnp.float32


def exchange(blocks, axes):
    return lax.all_to_all(blocks, axes, split_axis=0, concat_axis=0, tiled=True)


def neighbour_pairs():
    pairs = []
    for z in range(4):
        for xl in range(2):
            for core in range(2):
                for xh in range(2):
                    for y in range(4):
                        src = (((z * 2 + xl) * 2 + core) * 2 + xh) * 4 + y
                        dst = (((z * 2 + 1 - xl) * 2 + core) * 2 + 1 - xh) * 4 + y
                        pairs.append((src, dst))
    return pairs


def shift(block, step):
    return lax.ppermute(block, "y", [(i, (i + step) % 4) for i in range(4)])


def gather_pair(keys, values):
    pair = jnp.concatenate([keys, values], axis=1)
    blocks = [pair]
    for ahead in range(1, 8):
        pairs = []
        for index in range(8):
            xh, y = index // 4, index % 4
            pairs.append(((xh ^ (ahead // 4)) * 4 + (y + ahead) % 4, index))
        blocks.append(lax.ppermute(pair, CTX, pairs))
    return blocks


def attend_kernel(place_ref, query_ref, *refs):
    *block_refs, out_ref, bias, flipped, held = refs
    tok = query_ref.shape[0]
    heads = query_ref.shape[1] // DH

    @pl.when(pl.program_id(0) == 0)
    def _():
        query_pos = place_ref[0] * tok + lax.broadcasted_iota(jnp.int32, (tok, tok), 0)
        for ahead in range(8):
            high = place_ref[1] if ahead < 4 else 1 - place_ref[1]
            source = high * 4 + lax.rem(place_ref[2] + ahead, 4)
            key_pos = source * tok + lax.broadcasted_iota(jnp.int32, (tok, tok), 1)
            at = slice(ahead * tok, (ahead + 1) * tok)
            bias[:, at] = jnp.where(key_pos <= query_pos, 0.0, -1e30)
            flipped[:, at] = block_refs[2 * ahead][...].T
            held[at] = block_refs[2 * ahead + 1][...]

    for head in range(0, heads, 2):
        pair = [slice((head + i) * DH, (head + i + 1) * DH) for i in range(2)]
        rows = jnp.concatenate([query_ref[:, at] for at in pair], axis=0)
        scores = product(rows, flipped[...]) * DH ** (-0.5)
        scores = scores + jnp.concatenate([bias[...], bias[...]], axis=0)
        weights = jnp.exp(scores - jnp.max(scores, axis=1, keepdims=True))
        total = jnp.sum(weights, axis=1, keepdims=True)
        out = (product(weights.astype(BF), held[...]) / total).astype(BF)
        for i, at in enumerate(pair):
            out_ref[:, at] = out[i * tok : (i + 1) * tok]


def attend(place, queries, blocks, head):
    tok = queries.shape[0]
    keys = len(blocks) * tok
    half = queries.shape[1] // KVH
    block = 4 * DH
    steps = half // block
    specs = [
        pl.BlockSpec((tok, DH), lambda i, p: (0, head)),
        pl.BlockSpec((tok, DH), lambda i, p: (0, KVH + head)),
    ]
    return pl.pallas_call(
        attend_kernel,
        grid_spec=pltpu.PrefetchScalarGridSpec(
            num_scalar_prefetch=1,
            grid=(steps,),
            in_specs=[pl.BlockSpec((tok, block), lambda i, p: (0, head * steps + i))] + specs * len(blocks),
            out_specs=pl.BlockSpec((tok, block), lambda i, p: (0, i)),
            scratch_shapes=[
                pltpu.VMEM((tok, keys), F32), pltpu.VMEM((DH, keys), BF), pltpu.VMEM((keys, DH), BF)
            ],
        ),
        out_shape=jax.ShapeDtypeStruct((tok, half), BF),
        compiler_params=pltpu.CompilerParams(vmem_limit_bytes=16 * 1024 * 1024),
        cost_estimate=pl.CostEstimate(
            flops=4 * tok * half * keys, bytes_accessed=4 * tok * half, transcendentals=tok * half * 8
        ),
    )(place, queries, *[block for block in blocks for _ in range(2)])


def own_columns(left, right, weight_ref):
    half = left.shape[1]
    return product(left, weight_ref[:half]) + product(right, weight_ref[half:])


def pair_columns(left, right, core_ref, fetched_ref, other_ref):
    swap = core_ref[0] == 1
    out = product(jnp.where(swap, right, left), fetched_ref[...])
    return out + product(jnp.where(swap, left, right), other_ref[...])


def near_kernel(core_ref, *refs, count, paired):
    left = jnp.concatenate([ref[...] for ref in refs[0 : 2 * count : 2]], axis=0)
    right = jnp.concatenate([ref[...] for ref in refs[1 : 2 * count : 2]], axis=0)
    if paired:
        out = pair_columns(left, right, core_ref, *refs[2 * count : 2 * count + 2])
    else:
        out = own_columns(left, right, refs[2 * count])
    tok = refs[0].shape[0]
    for i, ref in enumerate(refs[-count:]):
        ref[...] = out[i * tok : (i + 1) * tok].astype(BF)


def far_kernel(core_ref, left_ref, right_ref, weight_ref, fetched_ref, other_ref, out_ref):
    left, right = left_ref[...], right_ref[...]
    step, wide = pl.program_id(0), weight_ref.shape[1]
    own = own_columns(left, right, weight_ref)
    pair = pair_columns(left, right, core_ref, fetched_ref, other_ref)
    for base, out in ((0, own), (PACK, pair)):
        out_ref[:, pl.ds(pl.multiple_of(base + step * wide, wide), wide)] = out.astype(BF)


def columns(body, core, rows, weight, out_specs, out_shape):
    flat = [part for pair in rows for part in pair]
    tok, half = flat[0].shape
    wide = weight[0].shape[1]
    count = len(rows) * tok
    return pl.pallas_call(
        body,
        grid=(wide // COLUMNS,),
        in_specs=[pl.BlockSpec(memory_space=pltpu.SMEM)]
        + [whole((tok, half))] * len(flat)
        + [pl.BlockSpec((w.shape[0], COLUMNS), lambda i: (0, i)) for w in weight],
        out_specs=out_specs,
        out_shape=out_shape,
        compiler_params=pltpu.CompilerParams(vmem_limit_bytes=24 * 1024 * 1024),
        cost_estimate=pl.CostEstimate(
            flops=4 * count * half * wide, bytes_accessed=4 * half * wide + 4 * count * half, transcendentals=0
        ),
    )(core, *flat, *weight)


def project(attended, out_weight):
    first, second = attended
    tok, half = first.shape
    core = lax.axis_index("core")
    mine = lax.dynamic_slice_in_dim(out_weight, core * half, half, axis=0)
    fetched = lax.ppermute(mine, ALL, neighbour_pairs())
    below_a, above_a = shift(first, 1), shift(first, -1)
    below_b, above_b = shift(second, 1), shift(second, -1)
    far_a = shift(below_a, 1)
    far_b = shift(above_b, -1)
    other = lax.ppermute(fetched, "core", [(0, 1), (1, 0)])
    near = [(first, second), (below_a, below_b), (above_a, above_b)]
    which = core.reshape(1)
    specs = [pl.BlockSpec((tok, COLUMNS), lambda i: (0, i))] * 3
    shapes = [jax.ShapeDtypeStruct((tok, PACK), BF)] * 3
    own_body = functools.partial(near_kernel, count=3, paired=False)
    pair_body = functools.partial(near_kernel, count=3, paired=True)
    own = columns(own_body, which, near, [out_weight], specs, shapes)
    above_own, below_own = shift(own[1], -1), shift(own[2], 1)
    pair = columns(pair_body, which, near, [fetched, other], specs, shapes)
    far = columns(
        far_kernel, which, [(far_a, far_b)], [out_weight, fetched, other],
        whole((tok, 2 * PACK)), jax.ShapeDtypeStruct((tok, 2 * PACK), BF),
    )
    from_far = shift(far, 2)
    above_pair, below_pair = shift(pair[1], -1), shift(pair[2], 1)
    return [own[0], pair[0], above_own, above_pair, from_far, below_own, below_pair]


def product(left, right):
    return jnp.dot(left, right, preferred_element_type=F32)


def shuffle(pieces, slots, packing):
    cut = lax.broadcasted_iota(jnp.int32, (128, 128), 0 if packing else 1)
    held = lax.broadcasted_iota(jnp.int32, (128, 128), 1 if packing else 0)
    expert, piece, slot = lax.div(cut, 8), lax.rem(lax.div(cut, slots), pieces), lax.rem(cut, slots)
    return ((piece * 16 + expert) * slots + slot == held).astype(F32).astype(BF)


def packed_rows(rows, pieces, slots):
    wide = WIDTH // pieces
    cut = jnp.concatenate([rows[:, wide * s : wide * (s + 1)] for s in range(pieces)], axis=0)
    return product(shuffle(pieces, slots, True), cut).astype(BF)


def whole_rows(packed, pieces, slots):
    cut = product(shuffle(pieces, slots, False), packed).astype(BF)
    return [cut[16 * slots * s : 16 * slots * (s + 1)] for s in range(pieces)]


def make_kernel(
    place_ref, here_own, here_pair, above_own, above_pair, far_ref, below_own, below_pair,
    hidden_ref, gain_ref, pick_ref, last_ref,
    out_ref, halves_ref, residual_ref, normed, last_rows,
):
    step = pl.program_id(0)

    @pl.when(step == 0)
    def _():
        far_parts = far_ref.at[:, :PACK], far_ref.at[:, PACK:]
        parts = (here_own, here_pair), (above_own, above_pair), far_parts, (below_own, below_pair)
        for ahead, refs in enumerate(parts):
            y = lax.rem(place_ref[2] + ahead, 4)
            for high, ref in zip((place_ref[1], 1 - place_ref[1]), refs, strict=True):
                at = pl.ds(pl.multiple_of((high * 4 + y) * PACK, PACK), PACK)
                residual_ref[:, at] = hidden_ref[:, at].astype(F32) + ref[...].astype(F32)
        residual = residual_ref[...]
        mean = jnp.mean(residual * residual, axis=1, keepdims=True)
        normed[...] = (residual * lax.rsqrt(mean + 1e-06) * gain_ref[...]).astype(BF)

        halves_ref[...] = jnp.concatenate([normed[:, :HALF], normed[:, HALF:]], axis=0)
        last_rows[...] = product(last_ref[...], normed[...]).astype(BF)

    out_ref[:, :HALF] = product(pick_ref[...], halves_ref[...]).astype(BF)
    for i in range(2):
        rows = last_rows[pl.ds(pl.multiple_of(step * 32 + 16 * i, 16), 16), :]
        out_ref[128 * i : 128 * (i + 1), HALF:] = packed_rows(rows, 8, 1)


def silu_product(gated, lifted):
    return (gated / (1.0 + jnp.exp(-gated)) * lifted).astype(BF)


def expert_kernel(got_ref, gate_ref, up_ref, down_ref, out_ref):
    groups = got_ref.shape[0] // 128
    with_last = got_ref.shape[1] > HALF
    low, high = [], []
    for g in range(groups):
        pieces = whole_rows(got_ref[128 * g : 128 * (g + 1), :HALF], 2, FOUR)
        low.append(pieces[0])
        high.append(pieces[1])
    if with_last:
        for g in range(groups):
            pieces = whole_rows(got_ref[128 * g : 128 * (g + 1), HALF:], 8, 1)
            low.append(jnp.concatenate(pieces[:4], axis=1))
            high.append(jnp.concatenate(pieces[4:], axis=1))
    low, high = jnp.concatenate(low, axis=0), jnp.concatenate(high, axis=0)
    gated = product(low, gate_ref[:HALF]) + product(high, gate_ref[HALF:])
    lifted = product(low, up_ref[:HALF]) + product(high, up_ref[HALF:])
    served = product(silu_product(gated, lifted), down_ref[...]).astype(BF)
    for g in range(groups):
        out_ref[128 * g : 128 * (g + 1), :HALF] = packed_rows(served[64 * g : 64 * (g + 1)], 2, FOUR)
    if with_last:
        for g in range(groups):
            at = 64 * groups + 16 * g
            out_ref[128 * g : 128 * (g + 1), HALF:] = packed_rows(served[at : at + 16], 8, 1)


def experts(got, w_gate, w_up, w_down):
    wide = got.shape[1]
    hid = w_gate.shape[1]
    rows = SLOTS * wide // WIDTH
    return pl.pallas_call(
        expert_kernel,
        grid=(SLOTS // TILE,),
        in_specs=[tiled((TILE, wide))]
        + [pl.BlockSpec(w.shape, lambda i: (0, 0), pipeline_mode=pl.Buffered(1)) for w in (w_gate, w_up, w_down)],
        out_specs=tiled((TILE, wide)),
        out_shape=jax.ShapeDtypeStruct((SLOTS, wide), BF),
        compiler_params=pltpu.CompilerParams(vmem_limit_bytes=60 * 1024 * 1024),
        cost_estimate=pl.CostEstimate(
            flops=6 * rows * WIDTH * hid, bytes_accessed=4 * SLOTS * wide + 6 * WIDTH * hid, transcendentals=rows * hid
        ),
    )(got, w_gate, w_up, w_down)


def finish_kernel(low_ref, high_ref, split_ref, back_ref, out_ref):
    step = pl.program_id(0)
    tok, wide = low_ref.shape
    sums = product(split_ref[...], back_ref[...])
    for piece, ref in enumerate((low_ref, high_ref)):
        part = sums[tok * piece : tok * (piece + 1)]
        at = pl.ds(pl.multiple_of(piece * HALF + step * wide, wide), wide)
        out_ref[:, at] = (ref[...] + part).astype(BF)


def whole(shape, index=(0, 0)):
    return pl.BlockSpec(shape, lambda i: index)


def tiled(shape):
    return pl.BlockSpec(shape, lambda i: (i, 0))


def prep_kernel(routes_ref, scores_ref, pick_ref, pick_rest_ref, pick_last_ref, split_ref, split_rest_ref, split_last_ref):
    tok = routes_ref.shape[0]
    scores = scores_ref[...]
    gates = scores / jnp.sum(scores, axis=1, keepdims=True)
    expert = lax.broadcasted_iota(jnp.int32, (tok, EXPERTS), 1)
    hit = jnp.zeros((tok, EXPERTS), F32)
    gate = jnp.zeros((tok, EXPERTS), F32)
    for k in range(TOP):
        named = routes_ref[:, k : k + 1] == expert
        hit = hit + jnp.where(named, 1.0, 0.0)
        gate = gate + jnp.where(named, gates[:, k : k + 1], 0.0)
    row = lax.broadcasted_iota(jnp.int32, (tok, tok), 0)
    col = lax.broadcasted_iota(jnp.int32, (tok, tok), 1)
    earlier = product(jnp.where(col < row, 1.0, 0.0).astype(BF), hit.astype(BF))
    rank = jnp.where(hit > 0.0, earlier, -1.0)

    placed = jnp.broadcast_to(rank.T[:, None, :], (EXPERTS, 8, tok))
    order = lax.broadcasted_iota(jnp.int32, (EXPERTS, 8, tok), 1)
    for start, ref in ((0, pick_ref), (FOUR, pick_rest_ref)):
        taken = placed == (lax.rem(order, FOUR) + start).astype(F32)
        for p in range(2):
            part = jnp.where(taken & (lax.div(order, FOUR) == p), 1.0, 0.0)
            ref[:, p * tok : (p + 1) * tok] = part.reshape(SLOTS, tok).astype(BF)
    pick_last_ref[...] = jnp.where(rank.T == float(FULL), 1.0, 0.0).astype(BF)

    lane = lax.broadcasted_iota(jnp.int32, (EXPERTS, SLOTS), 1)
    own = lax.broadcasted_iota(jnp.int32, (EXPERTS, SLOTS), 0)
    spread = jnp.where(lax.div(lane, 8) == own, 1.0, 0.0).astype(BF)
    weigh = product(gate.astype(BF), spread)
    ranks = product(rank.astype(BF), spread)
    order = lax.rem(lax.broadcasted_iota(jnp.int32, (tok, SLOTS), 1), 8)
    for start, ref in ((0, split_ref), (FOUR, split_rest_ref)):
        taken = ranks == (lax.rem(order, FOUR) + start).astype(F32)
        for p in range(2):
            part = jnp.where(taken & (lax.div(order, FOUR) == p), weigh, 0.0)
            ref[tok * p : tok * (p + 1)] = part.astype(BF)
    split_last_ref[...] = jnp.where(rank == float(FULL), gate, 0.0).astype(BF)


def prep(routes, scores):
    tok = routes.shape[0]
    shapes = [(SLOTS, 2 * tok), (SLOTS, 2 * tok), (EXPERTS, tok), (2 * tok, SLOTS), (2 * tok, SLOTS), (tok, EXPERTS)]
    vmem = pl.BlockSpec(memory_space=pltpu.VMEM)
    return pl.pallas_call(
        prep_kernel,
        name="prep",
        in_specs=[vmem] * 2,
        out_specs=[vmem] * len(shapes),
        out_shape=[jax.ShapeDtypeStruct(shape, BF) for shape in shapes],
        compiler_params=pltpu.CompilerParams(vmem_limit_bytes=24 * 1024 * 1024),
        cost_estimate=pl.CostEstimate(flops=2 * 10**8, bytes_accessed=3 * 10**6, transcendentals=0),
    )(routes, scores)


def layer(
    hidden,
    queries,
    keys,
    values,
    out_weight,
    norm_gain,
    routes,
    slot_scores,
    gate_weight,
    up_weight,
    down_weight,
):
    tok, _ = hidden.shape[1:]
    place = jnp.stack([lax.axis_index(CTX), lax.axis_index("xh"), lax.axis_index("y")])
    gathered = gather_pair(keys[0], values[0])
    first = attend(place, queries[0], gathered, 0)
    second = attend(place, queries[0], gathered, 1)

    pick, pick_rest, pick_last, split, split_rest, split_last = prep(routes[0], slot_scores[0])

    columns_home = project((first, second), out_weight)

    shape = jax.ShapeDtypeStruct
    weights = gate_weight[0], up_weight[0], down_weight[0]

    def swap(rows):
        wide = rows.shape[1]
        return exchange(rows.reshape(EXPERTS, 8, wide), ALL).reshape(SLOTS, wide)

    sent, halves, residual = pl.pallas_call(
        make_kernel,
        name="make",
        grid_spec=pltpu.PrefetchScalarGridSpec(
            num_scalar_prefetch=1,
            grid=(SLOTS // 256,),
            in_specs=[pl.BlockSpec(part.shape, lambda i, p: (0, 0)) for part in columns_home]
            + [
                pl.BlockSpec((tok, WIDTH), lambda i, p: (0, 0)),
                pl.BlockSpec((1, WIDTH), lambda i, p: (0, 0)),
                pl.BlockSpec((256, 2 * tok), lambda i, p: (i, 0)),
                pl.BlockSpec((EXPERTS, tok), lambda i, p: (0, 0)),
            ],
            out_specs=[
                pl.BlockSpec((256, FIRST), lambda i, p: (i, 0)),
                pl.BlockSpec((2 * tok, HALF), lambda i, p: (0, 0)),
                pl.BlockSpec((tok, WIDTH), lambda i, p: (0, 0)),
            ],
            scratch_shapes=[pltpu.VMEM((tok, WIDTH), BF), pltpu.VMEM((EXPERTS, WIDTH), BF)],
        ),
        out_shape=[shape((SLOTS, FIRST), BF), shape((2 * tok, HALF), BF), shape((tok, WIDTH), F32)],
        compiler_params=pltpu.CompilerParams(vmem_limit_bytes=50 * 1024 * 1024),
        cost_estimate=pl.CostEstimate(
            flops=4 * SLOTS * tok * HALF, bytes_accessed=SLOTS * FIRST * 2, transcendentals=0
        ),
    )(place, *columns_home, hidden[0], norm_gain.reshape(1, WIDTH), pick, pick_last)
    got = swap(sent)
    got_rest = swap(product(pick_rest, halves).astype(BF))
    back = swap(experts(got, *weights))
    back_rest = swap(experts(got_rest, *weights))

    sums = product(split, back[:, :HALF])
    base = residual + product(split_last, back[:, HALF:].reshape(EXPERTS, WIDTH))
    base = base + jnp.concatenate([sums[:tok], sums[tok:]], axis=1)
    steps = HALF // PACK
    out = pl.pallas_call(
        finish_kernel,
        name="finish",
        grid=(steps,),
        in_specs=[
            pl.BlockSpec((tok, PACK), lambda i: (0, i)),
            pl.BlockSpec((tok, PACK), lambda i: (0, i + steps)),
            whole((2 * tok, SLOTS)),
            pl.BlockSpec((SLOTS, PACK), lambda i: (0, i)),
        ],
        out_specs=whole((tok, WIDTH)),
        out_shape=shape((tok, WIDTH), BF),
        compiler_params=pltpu.CompilerParams(vmem_limit_bytes=24 * 1024 * 1024),
        cost_estimate=pl.CostEstimate(
            flops=4 * tok * SLOTS * HALF, bytes_accessed=SLOTS * HALF * 2 + tok * WIDTH * 6, transcendentals=0
        ),
    )(base, base, split_rest, back_rest)
    return out[None]


def solution(mesh):
    fine = Mesh(mesh.devices.reshape(4, 2, 2, 2, 4), ALL)
    return jax.shard_map(
        layer,
        mesh=fine,
        in_specs=(
            P(DP, CTX, None),
            P(DP, CTX, None),
            P(DP, CTX, None),
            P(DP, CTX, None),
            P(None, CTX),
            P(),
            P(DP, CTX, None),
            P(DP, CTX, None),
            P(ALL, None, None),
            P(ALL, None, None),
            P(ALL, None, None),
        ),
        out_specs=P(DP, CTX, None),
        check_vma=False,
    )
```

```python
import functools

import jax
import jax.numpy as jnp
from jax import lax
from jax.experimental import pallas as pl
from jax.experimental.pallas import tpu as pltpu
from jax.sharding import Mesh, PartitionSpec as P


HQ = 32
KVH = 2
DH = 128
TOP = 8
EXPERTS = 128
FULL = 8
SLOTS = EXPERTS * FULL
WIDTH = 4096
PACK = WIDTH // 8
FOUR = 4
HALF = WIDTH // 2
FIRST = HALF + PACK
TILE = 512
COLUMNS = 256

DP = ("z", "xl", "core")
CTX = ("xh", "y")
ALL = DP + CTX
BF = jnp.bfloat16
F32 = jnp.float32


def exchange(blocks, axes):
    return lax.all_to_all(blocks, axes, split_axis=0, concat_axis=0, tiled=True)


def neighbour_pairs():
    pairs = []
    for z in range(4):
        for xl in range(2):
            for core in range(2):
                for xh in range(2):
                    for y in range(4):
                        src = (((z * 2 + xl) * 2 + core) * 2 + xh) * 4 + y
                        dst = (((z * 2 + 1 - xl) * 2 + core) * 2 + 1 - xh) * 4 + y
                        pairs.append((src, dst))
    return pairs


def shift(block, step):
    return lax.ppermute(block, "y", [(i, (i + step) % 4) for i in range(4)])


def gather_pair(keys, values):
    pair = jnp.concatenate([keys, values], axis=1)
    blocks = [pair]
    for ahead in range(1, 8):
        pairs = []
        for index in range(8):
            xh, y = index // 4, index % 4
            pairs.append(((xh ^ (ahead // 4)) * 4 + (y + ahead) % 4, index))
        blocks.append(lax.ppermute(pair, CTX, pairs))
    return blocks


def attend_kernel(place_ref, query_ref, *refs, whose):
    *block_refs, out_ref, bias, flipped, held = refs
    tok = query_ref.shape[0]
    heads = query_ref.shape[1] // DH

    @pl.when(pl.program_id(0) == 0)
    def _():
        query_pos = place_ref[whose] * tok + lax.broadcasted_iota(jnp.int32, (tok, tok), 0)
        for ahead in range(8):
            high = place_ref[1] if ahead < 4 else 1 - place_ref[1]
            source = high * 4 + lax.rem(place_ref[2] + ahead, 4)
            key_pos = source * tok + lax.broadcasted_iota(jnp.int32, (tok, tok), 1)
            at = slice(ahead * tok, (ahead + 1) * tok)
            bias[:, at] = jnp.where(key_pos <= query_pos, 0.0, -1e30)
            flipped[:, at] = block_refs[2 * ahead][...].T
            held[at] = block_refs[2 * ahead + 1][...]

    for head in range(0, heads, 2):
        pair = [slice((head + i) * DH, (head + i + 1) * DH) for i in range(2)]
        rows = jnp.concatenate([query_ref[:, at] for at in pair], axis=0)
        scores = product(rows, flipped[...]) * DH ** (-0.5)
        scores = scores + jnp.concatenate([bias[...], bias[...]], axis=0)
        weights = jnp.exp(scores - jnp.max(scores, axis=1, keepdims=True))
        total = jnp.sum(weights, axis=1, keepdims=True)
        out = (product(weights.astype(BF), held[...]) / total).astype(BF)
        for i, at in enumerate(pair):
            out_ref[:, at] = out[i * tok : (i + 1) * tok]


def attend(place, queries, blocks, head, whose=0):
    tok = queries.shape[0]
    keys = len(blocks) * tok
    half = HQ * DH // KVH
    first = head * (queries.shape[1] // half - 1)
    block = 4 * DH
    steps = half // block
    specs = [
        pl.BlockSpec((tok, DH), lambda i, p: (0, head)),
        pl.BlockSpec((tok, DH), lambda i, p: (0, KVH + head)),
    ]
    return pl.pallas_call(
        functools.partial(attend_kernel, whose=whose),
        grid_spec=pltpu.PrefetchScalarGridSpec(
            num_scalar_prefetch=1,
            grid=(steps,),
            in_specs=[pl.BlockSpec((tok, block), lambda i, p: (0, first * steps + i))] + specs * len(blocks),
            out_specs=pl.BlockSpec((tok, block), lambda i, p: (0, i)),
            scratch_shapes=[
                pltpu.VMEM((tok, keys), F32), pltpu.VMEM((DH, keys), BF), pltpu.VMEM((keys, DH), BF)
            ],
        ),
        out_shape=jax.ShapeDtypeStruct((tok, half), BF),
        compiler_params=pltpu.CompilerParams(vmem_limit_bytes=16 * 1024 * 1024),
        cost_estimate=pl.CostEstimate(
            flops=4 * tok * half * keys, bytes_accessed=4 * tok * half, transcendentals=tok * half * 8
        ),
    )(place, queries, *[block for block in blocks for _ in range(2)])


def own_columns(left, right, weight_ref):
    half = left.shape[1]
    return product(left, weight_ref[:half]) + product(right, weight_ref[half:])


def pair_columns(left, right, core_ref, fetched_ref, other_ref):
    swap = core_ref[0] == 1
    out = product(jnp.where(swap, right, left), fetched_ref[...])
    return out + product(jnp.where(swap, left, right), other_ref[...])


def near_kernel(core_ref, *refs, count, paired):
    left = jnp.concatenate([ref[...] for ref in refs[0 : 2 * count : 2]], axis=0)
    right = jnp.concatenate([ref[...] for ref in refs[1 : 2 * count : 2]], axis=0)
    if paired:
        out = pair_columns(left, right, core_ref, *refs[2 * count : 2 * count + 2])
    else:
        out = own_columns(left, right, refs[2 * count])
    tok = refs[0].shape[0]
    for i, ref in enumerate(refs[-count:]):
        ref[...] = out[i * tok : (i + 1) * tok].astype(BF)


def far_kernel(core_ref, left_ref, right_ref, weight_ref, fetched_ref, other_ref, out_ref):
    left, right = left_ref[...], right_ref[...]
    step, wide = pl.program_id(0), weight_ref.shape[1]
    own = own_columns(left, right, weight_ref)
    pair = pair_columns(left, right, core_ref, fetched_ref, other_ref)
    for base, out in ((0, own), (PACK, pair)):
        out_ref[:, pl.ds(pl.multiple_of(base + step * wide, wide), wide)] = out.astype(BF)


def columns(body, core, rows, weight, out_specs, out_shape):
    flat = [part for pair in rows for part in pair]
    tok, half = flat[0].shape
    wide = weight[0].shape[1]
    count = len(rows) * tok
    return pl.pallas_call(
        body,
        grid=(wide // COLUMNS,),
        in_specs=[pl.BlockSpec(memory_space=pltpu.SMEM)]
        + [whole((tok, half))] * len(flat)
        + [pl.BlockSpec((w.shape[0], COLUMNS), lambda i: (0, i)) for w in weight],
        out_specs=out_specs,
        out_shape=out_shape,
        compiler_params=pltpu.CompilerParams(vmem_limit_bytes=24 * 1024 * 1024),
        cost_estimate=pl.CostEstimate(
            flops=4 * count * half * wide, bytes_accessed=4 * half * wide + 4 * count * half, transcendentals=0
        ),
    )(core, *flat, *weight)


def half_kernel(core_ref, in_ref, out_ref):
    out_ref[...] = in_ref[...]


def half_of(weight, core):
    rows, wide = weight.shape[0] // 2, weight.shape[1]
    steps = 4
    return pl.pallas_call(
        half_kernel,
        name="half",
        grid_spec=pltpu.PrefetchScalarGridSpec(
            num_scalar_prefetch=1,
            grid=(steps,),
            in_specs=[pl.BlockSpec((rows // steps, wide), lambda i, c: (c[0] * steps + i, 0))],
            out_specs=pl.BlockSpec((rows // steps, wide), lambda i, c: (i, 0)),
        ),
        out_shape=jax.ShapeDtypeStruct((rows, wide), BF),
        compiler_params=pltpu.CompilerParams(vmem_limit_bytes=16 * 1024 * 1024),
        cost_estimate=pl.CostEstimate(flops=0, bytes_accessed=4 * rows * wide, transcendentals=0),
    )(core, pltpu.with_memory_space_constraint(weight, pltpu.HBM))


def project(attended, far_second, out_weight):
    first, second = attended
    tok, _ = first.shape
    core = lax.axis_index("core")
    mine = half_of(out_weight, core.reshape(1))
    fetched = lax.ppermute(mine, ALL, neighbour_pairs())
    below_a, above_a = shift(first, 1), shift(first, -1)
    below_b, above_b = shift(second, 1), shift(second, -1)
    far_a = shift(below_a, 1)
    other = lax.ppermute(fetched, "core", [(0, 1), (1, 0)])
    near = [(first, second), (below_a, below_b), (above_a, above_b)]
    which = core.reshape(1)
    specs = [pl.BlockSpec((tok, COLUMNS), lambda i: (0, i))] * 3
    shapes = [jax.ShapeDtypeStruct((tok, PACK), BF)] * 3
    own_body = functools.partial(near_kernel, count=3, paired=False)
    pair_body = functools.partial(near_kernel, count=3, paired=True)
    own = columns(own_body, which, near, [out_weight], specs, shapes)
    above_own, below_own = shift(own[1], -1), shift(own[2], 1)
    pair = columns(pair_body, which, near, [fetched, other], specs, shapes)
    far = columns(
        far_kernel, which, [(far_a, far_second)], [out_weight, fetched, other],
        whole((tok, 2 * PACK)), jax.ShapeDtypeStruct((tok, 2 * PACK), BF),
    )
    from_far = shift(far, 2)
    above_pair, below_pair = shift(pair[1], -1), shift(pair[2], 1)
    return [own[0], pair[0], above_own, above_pair, from_far, below_own, below_pair]


def product(left, right):
    return jnp.dot(left, right, preferred_element_type=F32)


def shuffle(pieces, slots, packing):
    cut = lax.broadcasted_iota(jnp.int32, (128, 128), 0 if packing else 1)
    held = lax.broadcasted_iota(jnp.int32, (128, 128), 1 if packing else 0)
    expert, piece, slot = lax.div(cut, 8), lax.rem(lax.div(cut, slots), pieces), lax.rem(cut, slots)
    return ((piece * 16 + expert) * slots + slot == held).astype(F32).astype(BF)


def packed_rows(rows, pieces, slots):
    wide = WIDTH // pieces
    cut = jnp.concatenate([rows[:, wide * s : wide * (s + 1)] for s in range(pieces)], axis=0)
    return product(shuffle(pieces, slots, True), cut).astype(BF)


def whole_rows(packed, pieces, slots):
    cut = product(shuffle(pieces, slots, False), packed).astype(BF)
    return [cut[16 * slots * s : 16 * slots * (s + 1)] for s in range(pieces)]


def make_kernel(
    place_ref, here_own, here_pair, above_own, above_pair, far_ref, below_own, below_pair,
    hidden_ref, gain_ref, pick_ref, last_ref,
    out_ref, halves_ref, residual_ref, normed, last_rows,
):
    step = pl.program_id(0)

    @pl.when(step == 0)
    def _():
        far_parts = far_ref.at[:, :PACK], far_ref.at[:, PACK:]
        parts = (here_own, here_pair), (above_own, above_pair), far_parts, (below_own, below_pair)
        for ahead, refs in enumerate(parts):
            y = lax.rem(place_ref[2] + ahead, 4)
            for high, ref in zip((place_ref[1], 1 - place_ref[1]), refs, strict=True):
                at = pl.ds(pl.multiple_of((high * 4 + y) * PACK, PACK), PACK)
                residual_ref[:, at] = hidden_ref[:, at].astype(F32) + ref[...].astype(F32)
        residual = residual_ref[...]
        mean = jnp.mean(residual * residual, axis=1, keepdims=True)
        normed[...] = (residual * lax.rsqrt(mean + 1e-06) * gain_ref[...]).astype(BF)

        halves_ref[...] = jnp.concatenate([normed[:, :HALF], normed[:, HALF:]], axis=0)
        last_rows[...] = product(last_ref[...], normed[...]).astype(BF)

    out_ref[:, :HALF] = product(pick_ref[...], halves_ref[...]).astype(BF)
    for i in range(2):
        rows = last_rows[pl.ds(pl.multiple_of(step * 32 + 16 * i, 16), 16), :]
        out_ref[128 * i : 128 * (i + 1), HALF:] = packed_rows(rows, 8, 1)


def silu_product(gated, lifted):
    return (gated / (1.0 + jnp.exp(-gated)) * lifted).astype(BF)


def expert_kernel(got_ref, gate_ref, up_ref, down_ref, out_ref):
    groups = got_ref.shape[0] // 128
    with_last = got_ref.shape[1] > HALF
    low, high = [], []
    for g in range(groups):
        pieces = whole_rows(got_ref[128 * g : 128 * (g + 1), :HALF], 2, FOUR)
        low.append(pieces[0])
        high.append(pieces[1])
    if with_last:
        for g in range(groups):
            pieces = whole_rows(got_ref[128 * g : 128 * (g + 1), HALF:], 8, 1)
            low.append(jnp.concatenate(pieces[:4], axis=1))
            high.append(jnp.concatenate(pieces[4:], axis=1))
    low, high = jnp.concatenate(low, axis=0), jnp.concatenate(high, axis=0)
    gated = product(low, gate_ref[:HALF]) + product(high, gate_ref[HALF:])
    lifted = product(low, up_ref[:HALF]) + product(high, up_ref[HALF:])
    served = product(silu_product(gated, lifted), down_ref[...]).astype(BF)
    for g in range(groups):
        out_ref[128 * g : 128 * (g + 1), :HALF] = packed_rows(served[64 * g : 64 * (g + 1)], 2, FOUR)
    if with_last:
        for g in range(groups):
            at = 64 * groups + 16 * g
            out_ref[128 * g : 128 * (g + 1), HALF:] = packed_rows(served[at : at + 16], 8, 1)


def experts(got, w_gate, w_up, w_down):
    wide = got.shape[1]
    hid = w_gate.shape[1]
    rows = SLOTS * wide // WIDTH
    return pl.pallas_call(
        expert_kernel,
        grid=(SLOTS // TILE,),
        in_specs=[tiled((TILE, wide))]
        + [pl.BlockSpec(w.shape, lambda i: (0, 0), pipeline_mode=pl.Buffered(1)) for w in (w_gate, w_up, w_down)],
        out_specs=tiled((TILE, wide)),
        out_shape=jax.ShapeDtypeStruct((SLOTS, wide), BF),
        compiler_params=pltpu.CompilerParams(vmem_limit_bytes=60 * 1024 * 1024),
        cost_estimate=pl.CostEstimate(
            flops=6 * rows * WIDTH * hid, bytes_accessed=4 * SLOTS * wide + 6 * WIDTH * hid, transcendentals=rows * hid
        ),
    )(got, w_gate, w_up, w_down)


def finish_kernel(low_ref, high_ref, split_ref, back_ref, out_ref):
    step = pl.program_id(0)
    tok, wide = low_ref.shape
    sums = product(split_ref[...], back_ref[...])
    for piece, ref in enumerate((low_ref, high_ref)):
        part = sums[tok * piece : tok * (piece + 1)]
        at = pl.ds(pl.multiple_of(piece * HALF + step * wide, wide), wide)
        out_ref[:, at] = (ref[...] + part).astype(BF)


def whole(shape, index=(0, 0)):
    return pl.BlockSpec(shape, lambda i: index)


def tiled(shape):
    return pl.BlockSpec(shape, lambda i: (i, 0))


def prep_kernel(routes_ref, scores_ref, pick_ref, pick_rest_ref, pick_last_ref, split_ref, split_rest_ref, split_last_ref):
    tok = routes_ref.shape[0]
    scores = scores_ref[...]
    gates = scores / jnp.sum(scores, axis=1, keepdims=True)
    expert = lax.broadcasted_iota(jnp.int32, (tok, EXPERTS), 1)
    hit = jnp.zeros((tok, EXPERTS), F32)
    gate = jnp.zeros((tok, EXPERTS), F32)
    for k in range(TOP):
        named = routes_ref[:, k : k + 1] == expert
        hit = hit + jnp.where(named, 1.0, 0.0)
        gate = gate + jnp.where(named, gates[:, k : k + 1], 0.0)
    row = lax.broadcasted_iota(jnp.int32, (tok, tok), 0)
    col = lax.broadcasted_iota(jnp.int32, (tok, tok), 1)
    earlier = product(jnp.where(col < row, 1.0, 0.0).astype(BF), hit.astype(BF))
    rank = jnp.where(hit > 0.0, earlier, -1.0)

    placed = jnp.broadcast_to(rank.T[:, None, :], (EXPERTS, 8, tok))
    order = lax.broadcasted_iota(jnp.int32, (EXPERTS, 8, tok), 1)
    for start, ref in ((0, pick_ref), (FOUR, pick_rest_ref)):
        taken = placed == (lax.rem(order, FOUR) + start).astype(F32)
        for p in range(2):
            part = jnp.where(taken & (lax.div(order, FOUR) == p), 1.0, 0.0)
            ref[:, p * tok : (p + 1) * tok] = part.reshape(SLOTS, tok).astype(BF)
    pick_last_ref[...] = jnp.where(rank.T == float(FULL), 1.0, 0.0).astype(BF)

    lane = lax.broadcasted_iota(jnp.int32, (EXPERTS, SLOTS), 1)
    own = lax.broadcasted_iota(jnp.int32, (EXPERTS, SLOTS), 0)
    spread = jnp.where(lax.div(lane, 8) == own, 1.0, 0.0).astype(BF)
    weigh = product(gate.astype(BF), spread)
    ranks = product(rank.astype(BF), spread)
    order = lax.rem(lax.broadcasted_iota(jnp.int32, (tok, SLOTS), 1), 8)
    for start, ref in ((0, split_ref), (FOUR, split_rest_ref)):
        taken = ranks == (lax.rem(order, FOUR) + start).astype(F32)
        for p in range(2):
            part = jnp.where(taken & (lax.div(order, FOUR) == p), weigh, 0.0)
            ref[tok * p : tok * (p + 1)] = part.astype(BF)
    split_last_ref[...] = jnp.where(rank == float(FULL), gate, 0.0).astype(BF)


def prep(routes, scores):
    tok = routes.shape[0]
    shapes = [(SLOTS, 2 * tok), (SLOTS, 2 * tok), (EXPERTS, tok), (2 * tok, SLOTS), (2 * tok, SLOTS), (tok, EXPERTS)]
    vmem = pl.BlockSpec(memory_space=pltpu.VMEM)
    return pl.pallas_call(
        prep_kernel,
        name="prep",
        in_specs=[vmem] * 2,
        out_specs=[vmem] * len(shapes),
        out_shape=[jax.ShapeDtypeStruct(shape, BF) for shape in shapes],
        compiler_params=pltpu.CompilerParams(vmem_limit_bytes=24 * 1024 * 1024),
        cost_estimate=pl.CostEstimate(flops=2 * 10**8, bytes_accessed=3 * 10**6, transcendentals=0),
    )(routes, scores)


def layer(
    hidden,
    queries,
    keys,
    values,
    out_weight,
    norm_gain,
    routes,
    slot_scores,
    gate_weight,
    up_weight,
    down_weight,
):
    tok, _ = hidden.shape[1:]
    xh, y = lax.axis_index("xh"), lax.axis_index("y")
    place = jnp.stack([lax.axis_index(CTX), xh, y, xh * 4 + (y + 2) % 4])
    blocks = gather_pair(keys[0], values[0])
    far_query = shift(queries[0][:, WIDTH // 2 :], 2)
    near_query = pltpu.with_memory_space_constraint(queries[0], pltpu.HBM)
    first = attend(place, near_query, blocks, 0)
    second = attend(place, near_query, blocks, 1)
    far_second = attend(place, far_query, blocks, 1, 3)

    pick, pick_rest, pick_last, split, split_rest, split_last = prep(routes[0], slot_scores[0])

    columns_home = project((first, second), far_second, out_weight)

    shape = jax.ShapeDtypeStruct
    weights = gate_weight[0], up_weight[0], down_weight[0]

    def swap(rows):
        wide = rows.shape[1]
        return exchange(rows.reshape(EXPERTS, 8, wide), ALL).reshape(SLOTS, wide)

    sent, halves, residual = pl.pallas_call(
        make_kernel,
        name="make",
        grid_spec=pltpu.PrefetchScalarGridSpec(
            num_scalar_prefetch=1,
            grid=(SLOTS // 256,),
            in_specs=[pl.BlockSpec(part.shape, lambda i, p: (0, 0)) for part in columns_home]
            + [
                pl.BlockSpec((tok, WIDTH), lambda i, p: (0, 0)),
                pl.BlockSpec((1, WIDTH), lambda i, p: (0, 0)),
                pl.BlockSpec((256, 2 * tok), lambda i, p: (i, 0)),
                pl.BlockSpec((EXPERTS, tok), lambda i, p: (0, 0)),
            ],
            out_specs=[
                pl.BlockSpec((256, FIRST), lambda i, p: (i, 0)),
                pl.BlockSpec((2 * tok, HALF), lambda i, p: (0, 0)),
                pl.BlockSpec((tok, WIDTH), lambda i, p: (0, 0)),
            ],
            scratch_shapes=[pltpu.VMEM((tok, WIDTH), BF), pltpu.VMEM((EXPERTS, WIDTH), BF)],
        ),
        out_shape=[shape((SLOTS, FIRST), BF), shape((2 * tok, HALF), BF), shape((tok, WIDTH), F32)],
        compiler_params=pltpu.CompilerParams(vmem_limit_bytes=50 * 1024 * 1024),
        cost_estimate=pl.CostEstimate(
            flops=4 * SLOTS * tok * HALF, bytes_accessed=SLOTS * FIRST * 2, transcendentals=0
        ),
    )(place, *columns_home, hidden[0], norm_gain.reshape(1, WIDTH), pick, pick_last)
    got = swap(sent)
    got_rest = swap(product(pick_rest, halves).astype(BF))
    back = swap(experts(got, *weights))
    back_rest = swap(experts(got_rest, *weights))

    sums = product(split, back[:, :HALF])
    base = residual + product(split_last, back[:, HALF:].reshape(EXPERTS, WIDTH))
    base = base + jnp.concatenate([sums[:tok], sums[tok:]], axis=1)
    steps = HALF // PACK
    out = pl.pallas_call(
        finish_kernel,
        name="finish",
        grid=(steps,),
        in_specs=[
            pl.BlockSpec((tok, PACK), lambda i: (0, i)),
            pl.BlockSpec((tok, PACK), lambda i: (0, i + steps)),
            whole((2 * tok, SLOTS)),
            pl.BlockSpec((SLOTS, PACK), lambda i: (0, i)),
        ],
        out_specs=whole((tok, WIDTH)),
        out_shape=shape((tok, WIDTH), BF),
        compiler_params=pltpu.CompilerParams(vmem_limit_bytes=24 * 1024 * 1024),
        cost_estimate=pl.CostEstimate(
            flops=4 * tok * SLOTS * HALF, bytes_accessed=SLOTS * HALF * 2 + tok * WIDTH * 6, transcendentals=0
        ),
    )(base, base, split_rest, back_rest)
    return out[None]


def solution(mesh):
    fine = Mesh(mesh.devices.reshape(4, 2, 2, 2, 4), ALL)
    return jax.shard_map(
        layer,
        mesh=fine,
        in_specs=(
            P(DP, CTX, None),
            P(DP, CTX, None),
            P(DP, CTX, None),
            P(DP, CTX, None),
            P(None, CTX),
            P(),
            P(DP, CTX, None),
            P(DP, CTX, None),
            P(ALL, None, None),
            P(ALL, None, None),
            P(ALL, None, None),
        ),
        out_specs=P(DP, CTX, None),
        check_vma=False,
    )
```

```python
import functools

import jax
import jax.numpy as jnp
from jax import lax
from jax.experimental import pallas as pl
from jax.experimental.pallas import tpu as pltpu
from jax.sharding import Mesh, PartitionSpec as P


KVH = 2
DH = 128
TOP = 8
EXPERTS = 128
FULL = 8
SLOTS = EXPERTS * FULL
WIDTH = 4096
PACK = WIDTH // 8
FOUR = 4
HALF = WIDTH // 2
FIRST = HALF + PACK
TILE = 512
COLUMNS = 256

DP = ("z", "xl", "core")
CTX = ("xh", "y")
ALL = DP + CTX
BF = jnp.bfloat16
F32 = jnp.float32


def exchange(blocks, axes):
    return lax.all_to_all(blocks, axes, split_axis=0, concat_axis=0, tiled=True)


def neighbour_pairs():
    pairs = []
    for z in range(4):
        for xl in range(2):
            for core in range(2):
                for xh in range(2):
                    for y in range(4):
                        src = (((z * 2 + xl) * 2 + core) * 2 + xh) * 4 + y
                        dst = (((z * 2 + 1 - xl) * 2 + core) * 2 + 1 - xh) * 4 + y
                        pairs.append((src, dst))
    return pairs


def shift(block, step):
    return lax.ppermute(block, "y", [(i, (i + step) % 4) for i in range(4)])


def gather_pair(keys, values):
    pair = jnp.concatenate([keys, values], axis=1)
    blocks = [pair]
    for ahead in range(1, 8):
        pairs = []
        for index in range(8):
            xh, y = index // 4, index % 4
            pairs.append(((xh ^ (ahead // 4)) * 4 + (y + ahead) % 4, index))
        blocks.append(lax.ppermute(pair, CTX, pairs))
    return blocks


def attend_kernel(place_ref, query_ref, *refs):
    *block_refs, out_ref, bias, flipped, held = refs
    tok = query_ref.shape[0]
    heads = query_ref.shape[1] // DH

    @pl.when(pl.program_id(0) == 0)
    def _():
        query_pos = place_ref[0] * tok + lax.broadcasted_iota(jnp.int32, (tok, tok), 0)
        for ahead in range(8):
            high = place_ref[1] if ahead < 4 else 1 - place_ref[1]
            source = high * 4 + lax.rem(place_ref[2] + ahead, 4)
            key_pos = source * tok + lax.broadcasted_iota(jnp.int32, (tok, tok), 1)
            at = slice(ahead * tok, (ahead + 1) * tok)
            bias[:, at] = jnp.where(key_pos <= query_pos, 0.0, -1e30)
            flipped[:, at] = block_refs[2 * ahead][...].T
            held[at] = block_refs[2 * ahead + 1][...]

    for head in range(0, heads, 2):
        pair = [slice((head + i) * DH, (head + i + 1) * DH) for i in range(2)]
        rows = jnp.concatenate([query_ref[:, at] for at in pair], axis=0)
        scores = product(rows, flipped[...]) * DH ** (-0.5)
        scores = scores + jnp.concatenate([bias[...], bias[...]], axis=0)
        weights = jnp.exp(scores - jnp.max(scores, axis=1, keepdims=True))
        total = jnp.sum(weights, axis=1, keepdims=True)
        out = (product(weights.astype(BF), held[...]) / total).astype(BF)
        for i, at in enumerate(pair):
            out_ref[:, at] = out[i * tok : (i + 1) * tok]


def attend(place, queries, blocks, head):
    tok = queries.shape[0]
    keys = len(blocks) * tok
    half = queries.shape[1] // KVH
    block = 4 * DH
    steps = half // block
    specs = [
        pl.BlockSpec((tok, DH), lambda i, p: (0, head)),
        pl.BlockSpec((tok, DH), lambda i, p: (0, KVH + head)),
    ]
    return pl.pallas_call(
        attend_kernel,
        grid_spec=pltpu.PrefetchScalarGridSpec(
            num_scalar_prefetch=1,
            grid=(steps,),
            in_specs=[pl.BlockSpec((tok, block), lambda i, p: (0, head * steps + i))] + specs * len(blocks),
            out_specs=pl.BlockSpec((tok, block), lambda i, p: (0, i)),
            scratch_shapes=[
                pltpu.VMEM((tok, keys), F32), pltpu.VMEM((DH, keys), BF), pltpu.VMEM((keys, DH), BF)
            ],
        ),
        out_shape=jax.ShapeDtypeStruct((tok, half), BF),
        compiler_params=pltpu.CompilerParams(vmem_limit_bytes=16 * 1024 * 1024),
        cost_estimate=pl.CostEstimate(
            flops=4 * tok * half * keys, bytes_accessed=4 * tok * half, transcendentals=tok * half * 8
        ),
    )(place, queries, *[block for block in blocks for _ in range(2)])


def own_columns(left, right, weight_ref):
    half = left.shape[1]
    return product(left, weight_ref[:half]) + product(right, weight_ref[half:])


def pair_columns(left, right, core_ref, fetched_ref, other_ref):
    swap = core_ref[0] == 1
    out = product(jnp.where(swap, right, left), fetched_ref[...])
    return out + product(jnp.where(swap, left, right), other_ref[...])


def near_kernel(core_ref, *refs, count, paired):
    left = jnp.concatenate([ref[...] for ref in refs[0 : 2 * count : 2]], axis=0)
    right = jnp.concatenate([ref[...] for ref in refs[1 : 2 * count : 2]], axis=0)
    if paired:
        out = pair_columns(left, right, core_ref, *refs[2 * count : 2 * count + 2])
    else:
        out = own_columns(left, right, refs[2 * count])
    tok = refs[0].shape[0]
    for i, ref in enumerate(refs[-count:]):
        ref[...] = out[i * tok : (i + 1) * tok].astype(BF)


def far_kernel(core_ref, left_ref, right_ref, weight_ref, fetched_ref, other_ref, out_ref):
    left, right = left_ref[...], right_ref[...]
    step, wide = pl.program_id(0), weight_ref.shape[1]
    own = own_columns(left, right, weight_ref)
    pair = pair_columns(left, right, core_ref, fetched_ref, other_ref)
    for base, out in ((0, own), (PACK, pair)):
        out_ref[:, pl.ds(pl.multiple_of(base + step * wide, wide), wide)] = out.astype(BF)


def columns(body, core, rows, weight, out_specs, out_shape):
    flat = [part for pair in rows for part in pair]
    tok, half = flat[0].shape
    wide = weight[0].shape[1]
    count = len(rows) * tok
    return pl.pallas_call(
        body,
        grid=(wide // COLUMNS,),
        in_specs=[pl.BlockSpec(memory_space=pltpu.SMEM)]
        + [whole((tok, half))] * len(flat)
        + [pl.BlockSpec((w.shape[0], COLUMNS), lambda i: (0, i)) for w in weight],
        out_specs=out_specs,
        out_shape=out_shape,
        compiler_params=pltpu.CompilerParams(vmem_limit_bytes=24 * 1024 * 1024),
        cost_estimate=pl.CostEstimate(
            flops=4 * count * half * wide, bytes_accessed=4 * half * wide + 4 * count * half, transcendentals=0
        ),
    )(core, *flat, *weight)


def project(attended, out_weight):
    first, second = attended
    tok, half = first.shape
    core = lax.axis_index("core")
    mine = lax.dynamic_slice_in_dim(out_weight, core * half, half, axis=0)
    fetched = lax.ppermute(mine, ALL, neighbour_pairs())
    below_a, above_a = shift(first, 1), shift(first, -1)
    below_b, above_b = shift(second, 1), shift(second, -1)
    far_a = shift(below_a, 1)
    far_b = shift(above_b, -1)
    other = lax.ppermute(fetched, "core", [(0, 1), (1, 0)])
    near = [(first, second), (below_a, below_b), (above_a, above_b)]
    which = core.reshape(1)
    specs = [pl.BlockSpec((tok, COLUMNS), lambda i: (0, i))] * 3
    shapes = [jax.ShapeDtypeStruct((tok, PACK), BF)] * 3
    own_body = functools.partial(near_kernel, count=3, paired=False)
    pair_body = functools.partial(near_kernel, count=3, paired=True)
    own = columns(own_body, which, near, [out_weight], specs, shapes)
    above_own, below_own = shift(own[1], -1), shift(own[2], 1)
    pair = columns(pair_body, which, near, [fetched, other], specs, shapes)
    far = columns(
        far_kernel, which, [(far_a, far_b)], [out_weight, fetched, other],
        whole((tok, 2 * PACK)), jax.ShapeDtypeStruct((tok, 2 * PACK), BF),
    )
    from_far = shift(far, 2)
    above_pair, below_pair = shift(pair[1], -1), shift(pair[2], 1)
    return [own[0], pair[0], above_own, above_pair, from_far, below_own, below_pair]


def product(left, right):
    return jnp.dot(left, right, preferred_element_type=F32)


def shuffle(pieces, slots, packing):
    cut = lax.broadcasted_iota(jnp.int32, (128, 128), 0 if packing else 1)
    held = lax.broadcasted_iota(jnp.int32, (128, 128), 1 if packing else 0)
    expert, piece, slot = lax.div(cut, 8), lax.rem(lax.div(cut, slots), pieces), lax.rem(cut, slots)
    return ((piece * 16 + expert) * slots + slot == held).astype(F32).astype(BF)


def packed_rows(rows, pieces, slots):
    wide = WIDTH // pieces
    cut = jnp.concatenate([rows[:, wide * s : wide * (s + 1)] for s in range(pieces)], axis=0)
    return product(shuffle(pieces, slots, True), cut).astype(BF)


def whole_rows(packed, pieces, slots):
    cut = product(shuffle(pieces, slots, False), packed).astype(BF)
    return [cut[16 * slots * s : 16 * slots * (s + 1)] for s in range(pieces)]


def make_kernel(
    place_ref, here_own, here_pair, above_own, above_pair, far_ref, below_own, below_pair,
    hidden_ref, gain_ref, pick_ref, last_ref,
    out_ref, halves_ref, residual_ref, normed, last_rows,
):
    step = pl.program_id(0)

    @pl.when(step == 0)
    def _():
        far_parts = far_ref.at[:, :PACK], far_ref.at[:, PACK:]
        parts = (here_own, here_pair), (above_own, above_pair), far_parts, (below_own, below_pair)
        for ahead, refs in enumerate(parts):
            y = lax.rem(place_ref[2] + ahead, 4)
            for high, ref in zip((place_ref[1], 1 - place_ref[1]), refs, strict=True):
                at = pl.ds(pl.multiple_of((high * 4 + y) * PACK, PACK), PACK)
                residual_ref[:, at] = hidden_ref[:, at].astype(F32) + ref[...].astype(F32)
        residual = residual_ref[...]
        mean = jnp.mean(residual * residual, axis=1, keepdims=True)
        normed[...] = (residual * lax.rsqrt(mean + 1e-06) * gain_ref[...]).astype(BF)

        halves_ref[...] = jnp.concatenate([normed[:, :HALF], normed[:, HALF:]], axis=0)
        last_rows[...] = product(last_ref[...], normed[...]).astype(BF)

    out_ref[:, :HALF] = product(pick_ref[...], halves_ref[...]).astype(BF)
    for i in range(2):
        rows = last_rows[pl.ds(pl.multiple_of(step * 32 + 16 * i, 16), 16), :]
        out_ref[128 * i : 128 * (i + 1), HALF:] = packed_rows(rows, 8, 1)


def silu_product(gated, lifted):
    return (gated / (1.0 + jnp.exp(-gated)) * lifted).astype(BF)


def expert_kernel(got_ref, gate_ref, up_ref, down_ref, out_ref):
    groups = got_ref.shape[0] // 128
    with_last = got_ref.shape[1] > HALF
    low, high = [], []
    for g in range(groups):
        pieces = whole_rows(got_ref[128 * g : 128 * (g + 1), :HALF], 2, FOUR)
        low.append(pieces[0])
        high.append(pieces[1])
    if with_last:
        for g in range(groups):
            pieces = whole_rows(got_ref[128 * g : 128 * (g + 1), HALF:], 8, 1)
            low.append(jnp.concatenate(pieces[:4], axis=1))
            high.append(jnp.concatenate(pieces[4:], axis=1))
    low, high = jnp.concatenate(low, axis=0), jnp.concatenate(high, axis=0)
    gated = product(low, gate_ref[:HALF]) + product(high, gate_ref[HALF:])
    lifted = product(low, up_ref[:HALF]) + product(high, up_ref[HALF:])
    served = product(silu_product(gated, lifted), down_ref[...]).astype(BF)
    for g in range(groups):
        out_ref[128 * g : 128 * (g + 1), :HALF] = packed_rows(served[64 * g : 64 * (g + 1)], 2, FOUR)
    if with_last:
        for g in range(groups):
            at = 64 * groups + 16 * g
            out_ref[128 * g : 128 * (g + 1), HALF:] = packed_rows(served[at : at + 16], 8, 1)


def experts(got, w_gate, w_up, w_down):
    wide = got.shape[1]
    hid = w_gate.shape[1]
    rows = SLOTS * wide // WIDTH
    return pl.pallas_call(
        expert_kernel,
        grid=(SLOTS // TILE,),
        in_specs=[tiled((TILE, wide))]
        + [pl.BlockSpec(w.shape, lambda i: (0, 0), pipeline_mode=pl.Buffered(1)) for w in (w_gate, w_up, w_down)],
        out_specs=tiled((TILE, wide)),
        out_shape=jax.ShapeDtypeStruct((SLOTS, wide), BF),
        compiler_params=pltpu.CompilerParams(vmem_limit_bytes=60 * 1024 * 1024),
        cost_estimate=pl.CostEstimate(
            flops=6 * rows * WIDTH * hid, bytes_accessed=4 * SLOTS * wide + 6 * WIDTH * hid, transcendentals=rows * hid
        ),
    )(got, w_gate, w_up, w_down)


def finish_kernel(low_ref, high_ref, split_ref, back_ref, out_ref):
    step = pl.program_id(0)
    tok, wide = low_ref.shape
    sums = product(split_ref[...], back_ref[...])
    for piece, ref in enumerate((low_ref, high_ref)):
        part = sums[tok * piece : tok * (piece + 1)]
        at = pl.ds(pl.multiple_of(piece * HALF + step * wide, wide), wide)
        out_ref[:, at] = (ref[...] + part).astype(BF)


def whole(shape, index=(0, 0)):
    return pl.BlockSpec(shape, lambda i: index)


def tiled(shape):
    return pl.BlockSpec(shape, lambda i: (i, 0))


def prep_kernel(routes_ref, scores_ref, pick_ref, pick_rest_ref, pick_last_ref, split_ref, split_rest_ref, split_last_ref):
    tok = routes_ref.shape[0]
    scores = scores_ref[...]
    gates = scores / jnp.sum(scores, axis=1, keepdims=True)
    expert = lax.broadcasted_iota(jnp.int32, (tok, EXPERTS), 1)
    hit = jnp.zeros((tok, EXPERTS), F32)
    gate = jnp.zeros((tok, EXPERTS), F32)
    for k in range(TOP):
        named = routes_ref[:, k : k + 1] == expert
        hit = hit + jnp.where(named, 1.0, 0.0)
        gate = gate + jnp.where(named, gates[:, k : k + 1], 0.0)
    row = lax.broadcasted_iota(jnp.int32, (tok, tok), 0)
    col = lax.broadcasted_iota(jnp.int32, (tok, tok), 1)
    earlier = product(jnp.where(col < row, 1.0, 0.0).astype(BF), hit.astype(BF))
    rank = jnp.where(hit > 0.0, earlier, -1.0)

    placed = jnp.broadcast_to(rank.T[:, None, :], (EXPERTS, 8, tok))
    order = lax.broadcasted_iota(jnp.int32, (EXPERTS, 8, tok), 1)
    for start, ref in ((0, pick_ref), (FOUR, pick_rest_ref)):
        taken = placed == (lax.rem(order, FOUR) + start).astype(F32)
        for p in range(2):
            part = jnp.where(taken & (lax.div(order, FOUR) == p), 1.0, 0.0)
            ref[:, p * tok : (p + 1) * tok] = part.reshape(SLOTS, tok).astype(BF)
    pick_last_ref[...] = jnp.where(rank.T == float(FULL), 1.0, 0.0).astype(BF)

    lane = lax.broadcasted_iota(jnp.int32, (EXPERTS, SLOTS), 1)
    own = lax.broadcasted_iota(jnp.int32, (EXPERTS, SLOTS), 0)
    spread = jnp.where(lax.div(lane, 8) == own, 1.0, 0.0).astype(BF)
    weigh = product(gate.astype(BF), spread)
    ranks = product(rank.astype(BF), spread)
    order = lax.rem(lax.broadcasted_iota(jnp.int32, (tok, SLOTS), 1), 8)
    for start, ref in ((0, split_ref), (FOUR, split_rest_ref)):
        taken = ranks == (lax.rem(order, FOUR) + start).astype(F32)
        for p in range(2):
            part = jnp.where(taken & (lax.div(order, FOUR) == p), weigh, 0.0)
            ref[tok * p : tok * (p + 1)] = part.astype(BF)
    split_last_ref[...] = jnp.where(rank == float(FULL), gate, 0.0).astype(BF)


def prep(routes, scores):
    tok = routes.shape[0]
    shapes = [(SLOTS, 2 * tok), (SLOTS, 2 * tok), (EXPERTS, tok), (2 * tok, SLOTS), (2 * tok, SLOTS), (tok, EXPERTS)]
    vmem = pl.BlockSpec(memory_space=pltpu.VMEM)
    return pl.pallas_call(
        prep_kernel,
        name="prep",
        in_specs=[vmem] * 2,
        out_specs=[vmem] * len(shapes),
        out_shape=[jax.ShapeDtypeStruct(shape, BF) for shape in shapes],
        compiler_params=pltpu.CompilerParams(vmem_limit_bytes=24 * 1024 * 1024),
        cost_estimate=pl.CostEstimate(flops=2 * 10**8, bytes_accessed=3 * 10**6, transcendentals=0),
    )(routes, scores)


def layer(
    hidden,
    queries,
    keys,
    values,
    out_weight,
    norm_gain,
    routes,
    slot_scores,
    gate_weight,
    up_weight,
    down_weight,
):
    tok, _ = hidden.shape[1:]
    place = jnp.stack([lax.axis_index(CTX), lax.axis_index("xh"), lax.axis_index("y")])
    gathered = gather_pair(keys[0], values[0])
    held = pltpu.with_memory_space_constraint(queries[0], pltpu.HBM)
    first = attend(place, held, gathered, 0)
    second = attend(place, held, gathered, 1)

    pick, pick_rest, pick_last, split, split_rest, split_last = prep(routes[0], slot_scores[0])

    columns_home = project((first, second), out_weight)

    shape = jax.ShapeDtypeStruct
    weights = gate_weight[0], up_weight[0], down_weight[0]

    def swap(rows):
        wide = rows.shape[1]
        return exchange(rows.reshape(EXPERTS, 8, wide), ALL).reshape(SLOTS, wide)

    sent, halves, residual = pl.pallas_call(
        make_kernel,
        name="make",
        grid_spec=pltpu.PrefetchScalarGridSpec(
            num_scalar_prefetch=1,
            grid=(SLOTS // 256,),
            in_specs=[pl.BlockSpec(part.shape, lambda i, p: (0, 0)) for part in columns_home]
            + [
                pl.BlockSpec((tok, WIDTH), lambda i, p: (0, 0)),
                pl.BlockSpec((1, WIDTH), lambda i, p: (0, 0)),
                pl.BlockSpec((256, 2 * tok), lambda i, p: (i, 0)),
                pl.BlockSpec((EXPERTS, tok), lambda i, p: (0, 0)),
            ],
            out_specs=[
                pl.BlockSpec((256, FIRST), lambda i, p: (i, 0)),
                pl.BlockSpec((2 * tok, HALF), lambda i, p: (0, 0)),
                pl.BlockSpec((tok, WIDTH), lambda i, p: (0, 0)),
            ],
            scratch_shapes=[pltpu.VMEM((tok, WIDTH), BF), pltpu.VMEM((EXPERTS, WIDTH), BF)],
        ),
        out_shape=[shape((SLOTS, FIRST), BF), shape((2 * tok, HALF), BF), shape((tok, WIDTH), F32)],
        compiler_params=pltpu.CompilerParams(vmem_limit_bytes=50 * 1024 * 1024),
        cost_estimate=pl.CostEstimate(
            flops=4 * SLOTS * tok * HALF, bytes_accessed=SLOTS * FIRST * 2, transcendentals=0
        ),
    )(place, *columns_home, hidden[0], norm_gain.reshape(1, WIDTH), pick, pick_last)
    got = swap(sent)
    got_rest = swap(product(pick_rest, halves).astype(BF))
    back = swap(experts(got, *weights))
    back_rest = swap(experts(got_rest, *weights))

    sums = product(split, back[:, :HALF])
    base = residual + product(split_last, back[:, HALF:].reshape(EXPERTS, WIDTH))
    base = base + jnp.concatenate([sums[:tok], sums[tok:]], axis=1)
    steps = HALF // PACK
    out = pl.pallas_call(
        finish_kernel,
        name="finish",
        grid=(steps,),
        in_specs=[
            pl.BlockSpec((tok, PACK), lambda i: (0, i)),
            pl.BlockSpec((tok, PACK), lambda i: (0, i + steps)),
            whole((2 * tok, SLOTS)),
            pl.BlockSpec((SLOTS, PACK), lambda i: (0, i)),
        ],
        out_specs=whole((tok, WIDTH)),
        out_shape=shape((tok, WIDTH), BF),
        compiler_params=pltpu.CompilerParams(vmem_limit_bytes=24 * 1024 * 1024),
        cost_estimate=pl.CostEstimate(
            flops=4 * tok * SLOTS * HALF, bytes_accessed=SLOTS * HALF * 2 + tok * WIDTH * 6, transcendentals=0
        ),
    )(base, base, split_rest, back_rest)
    return out[None]


def solution(mesh):
    fine = Mesh(mesh.devices.reshape(4, 2, 2, 2, 4), ALL)
    return jax.shard_map(
        layer,
        mesh=fine,
        in_specs=(
            P(DP, CTX, None),
            P(DP, CTX, None),
            P(DP, CTX, None),
            P(DP, CTX, None),
            P(None, CTX),
            P(),
            P(DP, CTX, None),
            P(DP, CTX, None),
            P(ALL, None, None),
            P(ALL, None, None),
            P(ALL, None, None),
        ),
        out_specs=P(DP, CTX, None),
        check_vma=False,
    )
```
